32 devices in a mesh: seq: 16 (over z, x, core), head: 2 (over y).
Axes of the slice: x: 2, y: 2, z: 4, core: 2. Of those that a mesh axis runs over, the one named last changes fastest.
Arguments:
- queries: bfloat16 [2048, 4096], P('seq', 'head'), may hold values from -6 to 6, as said below
- keys: bfloat16 [2048, 4096], P('seq', 'head'), may hold values from -6 to 6, as said below
- values: bfloat16 [2048, 4096], P('seq', 'head'), may hold values from -6 to 6
- transitions: bfloat16 [2048, 4096], P('seq', 'head'), may hold values from -6 to 6, as said below
- betas: bfloat16 [2048, 32], P('seq', 'head'), may hold values from 0.19921875 to 1.5
- segments: int32 [2048], replicated, may hold values from 0 to 3, never falling along the last dimension, each value on 1 to 1024 neighbouring positions
- visits: int32 [16, 3], P('seq'), may hold values 0 or 1
Outputs:
- attended: bfloat16 [2048, 4096], P('seq', 'head')
The draws below stay inside these ranges and needn't reach their ends.
Inputs may be any that keep to these rules, and one draw needn't show every extreme that they name: `queries`: real-valued entries. `keys`: real-valued entries. `transitions`: real-valued entries, no head row all zero.
All inputs are finite; a program needn't handle non-finite values. No bound on the sum of `visits` on one device may be relied on, other than what follows from the above.
Results may differ from the reference program's by a relative error of at most 0.0036.
Values may be sent and summed in bfloat16 or wider, within the bound.
A program may use at most 64 MiB of HBM per device.

```python
import math
import jax
import jax.numpy as jnp
import numpy as np
from jax import lax

HEADS = 32
HEAD_DIM = 128
TOK_DEV = 128
BACK = 3
BLOCKS = 16
TOKENS = 2048
DOCS = 4


def base_draw(key, salt):
    noise_key = jax.random.fold_in(key, salt)
    return jnp.clip(jax.random.normal(noise_key, (TOKENS, HEADS * HEAD_DIM), jnp.float32), -4.0, 4.0)


def draw_queries(key, part):
    tensor = base_draw(key, 11)
    return tensor.astype(jnp.bfloat16)


def draw_keys(key, part):
    tensor = base_draw(key, 23)
    return tensor.astype(jnp.bfloat16)


def draw_transitions(key, part):
    tensor = base_draw(key, 37)
    return tensor.astype(jnp.bfloat16)


def touch_ends(result, own_key, low, high):
    shape = result.shape
    spot = [jax.random.randint(jax.random.fold_in(own_key, axis), (), 0, shape[axis]) for axis in range(len(shape))]
    result = result.at[tuple(spot)].set(low)
    longest = shape.index(max(shape))
    spot[longest] = (spot[longest] + 1) % shape[longest]
    return result.at[tuple(spot)].set(high)


def block_scale(key, extent, shards, smallest, largest):
    gain = 1.0
    for dim, blocks in shards:
        draws = jax.random.uniform(jax.random.fold_in(jax.random.fold_in(key, 6), dim), (blocks,), jnp.float32, smallest / len(shards), largest / len(shards))
        gain = gain * jnp.repeat(jnp.exp(draws), extent[dim] // blocks).reshape((-1,) + (1,) * (len(extent) - 1 - dim))
    return gain


def profile(amount, total, limit, lean):
    loads = [(1 << 20) // math.isqrt(grade ** lean) + 1 for grade in range(2, amount + 1)]
    rest, counts = total - limit - (amount - 1), [1] * (amount - 1)
    while rest > 0:
        movable = [i for i in range(amount - 1) if counts[i] < limit]
        whole, budget = sum([loads[i] for i in movable]), rest
        for i in movable:
            addition = min(limit - counts[i], max(1, budget * loads[i] // whole), rest)
            counts[i] = counts[i] + addition
            rest = rest - addition
    return np.array([limit] + counts)


def uneven_parts(rng, amount, total, limit, slope):
    if amount == 2:
        one = jax.random.randint(rng, (), max(1, total - limit), min(limit, total - 1) + 1)
        return jnp.stack([one, total - one])
    lengths = jnp.asarray(profile(amount, total, limit, slope), jnp.int32)
    pairs = (amount - 1) // 2
    donor, sink = lengths[1:1 + 2 * pairs:2], lengths[2:2 + 2 * pairs:2]
    room = jnp.minimum(donor - 1, limit - sink)
    passed = jax.random.randint(jax.random.fold_in(rng, 1), (pairs,), 0, 1 << 20) % (room + 1)
    lengths = lengths.at[1:1 + 2 * pairs:2].set(donor - passed).at[2:2 + 2 * pairs:2].set(sink + passed)
    return lengths[jax.random.permutation(jax.random.fold_in(rng, 2), amount)]


def scatter_about(rng, extent, scale, bound, cuts=(), kind=jnp.bfloat16):
    entries = jax.random.normal(rng, extent, jnp.float32) * scale
    if len(cuts) > 0:
        entries = block_scale(rng, extent, cuts, -0.22, 0.18) * entries
    return jnp.clip(entries, min=-bound, max=bound).astype(kind)


def setup_inputs(seed: int = 0) -> dict:
    splits = jax.random.split(jax.random.key(seed), 8)
    return {
        "queries": draw_queries(jax.random.fold_in(splits[7], 71), 0),
        "keys": draw_keys(jax.random.fold_in(splits[7], 71), 0),
        "values": scatter_about(splits[2], (TOKENS, HEADS * HEAD_DIM), 1.0, 6.0, ((0, 16), (1, 2))),
        "transitions": draw_transitions(jax.random.fold_in(splits[7], 71), 0),
        "betas": jnp.clip(jnp.exp(math.log(1.5) - 2.018817 * jax.random.uniform(splits[4], (TOKENS, HEADS), jnp.float32) ** block_scale(splits[4], (TOKENS, HEADS), ((0, 16), (1, 2)), -0.2, 0.2)), 0.19921875, 1.5).astype(jnp.bfloat16),
        "segments": jnp.searchsorted(jnp.cumsum(uneven_parts(splits[5], DOCS, TOKENS, min(8 * TOK_DEV, TOKENS // 2), 2)), jnp.arange(TOKENS), side="right").astype(jnp.int32),
        "visits": touch_ends((jax.random.randint(splits[6], (BLOCKS, BACK), 0, 4) < 3).astype(jnp.int32), jax.random.fold_in(splits[6], 1), 0, 1),
    }


HIGHEST = lax.Precision.HIGHEST
EPSILON = 1e-06

def heads_first(block, head_count):
    height = block.shape[0]
    return jnp.transpose(block.reshape(height, head_count, -1), (1, 0, 2))

def transition_parts(key_rows, raw_w, strength):
    length = key_rows.shape[1]
    width = key_rows.shape[2]
    unit_w = raw_w / jnp.sqrt(lax.optimization_barrier(jnp.sum(raw_w * raw_w, axis=-1, keepdims=True)) + EPSILON)
    strict = jnp.tril(jnp.ones((length, length), jnp.float32), -1)
    gram_mat = jnp.einsum('htd,hsd->hts', unit_w, unit_w, precision=HIGHEST)
    lower_mat = jnp.eye(length, dtype=jnp.float32)[None] + strict[None] * strength[:, :, None] * gram_mat
    cross_terms = jnp.einsum('htd,hjd->htj', unit_w, key_rows, precision=HIGHEST)
    right_side = jnp.concatenate([strength[:, :, None] * unit_w, strict[None] * strength[:, :, None] * cross_terms], axis=-1)
    solved = lax.linalg.triangular_solve(lower_mat, right_side, left_side=True, lower=True, unit_diagonal=True)
    back_rows = solved[:, :, :width]
    carry_coef = solved[:, :, width:]
    carried = key_rows - jnp.einsum('htj,htd->hjd', carry_coef, unit_w, precision=HIGHEST)
    return (unit_w, back_rows, carry_coef, carried)

def query_parts(query_rows, key_rows, unit_w, back_rows, carry_coef):
    length = query_rows.shape[1]
    inclusive = jnp.tril(jnp.ones((length, length), jnp.float32))
    query_w = jnp.einsum('hid,htd->hit', query_rows, unit_w, precision=HIGHEST) * inclusive[None]
    turned = query_rows - jnp.einsum('hit,htd->hid', query_w, back_rows, precision=HIGHEST)
    own_scores = jnp.einsum('hid,hjd->hij', query_rows, key_rows, precision=HIGHEST)
    own_scores = own_scores - jnp.einsum('hit,htj->hij', query_w, carry_coef, precision=HIGHEST)
    return (turned, own_scores)

def advance(carried, back_rows, unit_w):
    inner = jnp.einsum('hjd,htd->hjt', carried, back_rows, precision=HIGHEST)
    return carried - jnp.einsum('hjt,htd->hjd', inner, unit_w, precision=HIGHEST)

def weights_of(turned, own_scores, far_keys, seg_keys, seg_query, visit_row):
    length = own_scores.shape[1]
    cross_terms = jnp.einsum('hid,hjd->hij', turned, far_keys, precision=HIGHEST)
    scores = jnp.concatenate([cross_terms, own_scores], axis=-1) * HEAD_DIM ** (-0.5)
    spread = scores.shape[2]
    visited = jnp.concatenate([visit_row[::-1], jnp.ones((1,), jnp.int32)])
    visited = jnp.repeat(visited, length, total_repeat_length=spread)
    column = jnp.arange(spread, dtype=jnp.int32)
    row_ids = jnp.arange(length, dtype=jnp.int32)
    allowed = (visited[None, :] > 0) & (seg_keys[None, :] == seg_query[:, None])
    allowed = allowed & (column[None, :] <= row_ids[:, None] + (spread - length))
    scores = jnp.where(allowed[None], scores, -1e+30)
    row_max = lax.optimization_barrier(jnp.max(scores, axis=-1, keepdims=True))
    weights = jnp.exp(scores - row_max)
    total_w = lax.optimization_barrier(jnp.sum(weights, axis=-1, keepdims=True))
    return (weights.astype(jnp.bfloat16), total_w)

def reference(queries, keys, values, transitions, betas, segments, visits):
    length = TOK_DEV

    def by_block(tensor):
        return tensor.reshape(BLOCKS, length, tensor.shape[1])
    query_blocks = by_block(queries)
    key_blocks = by_block(keys)
    value_blocks = by_block(values)
    trans_blocks = by_block(transitions)
    beta_blocks = by_block(betas)

    def prepare(pieces):
        key_part, trans_part, beta_part = pieces
        unit_w, back_rows, carry_coef, carried = transition_parts(heads_first(key_part.astype(jnp.float32), HEADS), heads_first(trans_part.astype(jnp.float32), HEADS), beta_part.astype(jnp.float32).T)
        return (unit_w, back_rows, carried)
    units, backs, carried_all = lax.map(prepare, (key_blocks, trans_blocks, beta_blocks))
    moving = carried_all
    carried_list = []
    for distance in range(BACK):
        moving = jnp.concatenate([jnp.zeros_like(moving[:1]), moving[:-1]], axis=0)
        carried_list.append(moving)
        if distance + 1 < BACK:
            moving = jax.vmap(advance)(moving, backs, units)
    near_keys = jnp.concatenate(carried_list[::-1], axis=2)
    value_pad = jnp.concatenate([jnp.zeros((BACK * length, values.shape[1]), jnp.bfloat16), values], axis=0)
    segment_pad = jnp.concatenate([jnp.full((BACK * length,), -1, jnp.int32), segments.astype(jnp.int32)])

    def finish(pieces):
        block_index, query_part, key_part, trans_part, beta_part, far_keys = pieces
        key_rows = heads_first(key_part.astype(jnp.float32), HEADS)
        unit_w, back_rows, carry_coef, carried = transition_parts(key_rows, heads_first(trans_part.astype(jnp.float32), HEADS), beta_part.astype(jnp.float32).T)
        turned, own_scores = query_parts(heads_first(query_part.astype(jnp.float32), HEADS), key_rows, unit_w, back_rows, carry_coef)
        start = (block_index * length).astype(jnp.int32)
        seg_keys = lax.dynamic_slice_in_dim(segment_pad, start, (BACK + 1) * length)
        value_rows = lax.dynamic_slice_in_dim(value_pad, start, (BACK + 1) * length)
        visit_row = lax.dynamic_index_in_dim(visits, block_index, 0, keepdims=False).astype(jnp.int32)
        weights, total_w = weights_of(turned, own_scores, far_keys, seg_keys, seg_keys[BACK * length:], visit_row)
        mixed = jnp.einsum('hij,hjd->hid', weights.astype(jnp.float32), heads_first(value_rows, HEADS).astype(jnp.float32), precision=HIGHEST) / total_w
        return jnp.transpose(mixed, (1, 0, 2)).reshape(length, -1).astype(jnp.bfloat16)
    results = lax.map(finish, (jnp.arange(BLOCKS, dtype=jnp.int32), query_blocks, key_blocks, trans_blocks, beta_blocks, near_keys))
    return results.reshape(TOKENS, -1)
```

```python
import functools

import jax
import jax.numpy as jnp
from jax import lax
from jax.experimental import pallas as pl
from jax.experimental.pallas import tpu as pltpu
from jax.sharding import PartitionSpec as P

EPSILON = 1e-06
MESH = pl.DeviceIdType.MESH
F32 = jnp.float32
BF16 = jnp.bfloat16


def nn(a, b):
    return lax.dot_general(a, b, (((1,), (0,)), ((), ())), preferred_element_type=F32)


def nt(a, b):
    return lax.dot_general(a, b, (((1,), (1,)), ((), ())), preferred_element_type=F32)


def split(x):
    hi = x.astype(BF16)
    return hi, (x - hi.astype(F32)).astype(BF16)


def wide(*parts):
    return jnp.concatenate(parts, axis=1)


def tall(*parts):
    return jnp.concatenate(parts, axis=0)


def kernel(
    blocks, heads, group, sub, q_hbm, k_hbm, v_hbm, w_hbm, beta_ref, seg_ref, visit_ref, out_ref,
    q_ref, k_ref, v_ref, w_ref,
    far_in, far_out, val_in, relay_buf, back, coef, rnorm, beta_rows, turned, own, bias,
    far_send, far_recv, own_send, val_recv, relay_send, relay_recv,
    pair_send, pair_recv, skip_sems, load_sem,
):
    length = q_ref.shape[0]
    width = q_ref.shape[1] // heads
    depth = far_in.shape[0]
    groups = heads // group
    scale = width ** (-0.5)
    me = lax.axis_index("seq")
    odd = lax.rem(me, 2) == 1
    even = lax.rem(me, 2) == 0
    chip = lax.div(me, 2)
    chips = blocks // 2
    near_side = lax.rem(chip, 2) == 0
    far_side = lax.rem(chip, 2) == 1
    has_left = me >= 1
    has_right = me + 1 < blocks
    onward = chip + 1 < chips
    bent = odd & far_side & onward
    skips = odd & (chip + 2 < chips)
    relays = skips & near_side
    follows = even & (chip >= 1)
    skipped = even & (chip >= 2)

    loads = [
        pltpu.make_async_copy(src, dst, load_sem.at[i])
        for i, (src, dst) in enumerate(
            ((w_hbm, w_ref), (k_hbm, k_ref), (q_hbm, q_ref), (v_hbm, v_ref))
        )
    ]
    loads[0].start()
    loads[1].start()

    barrier = pltpu.get_barrier_semaphore()

    def greet(cond, other):
        @pl.when(cond)
        def _():
            pl.semaphore_signal(barrier, inc=1, device_id={"seq": other}, device_id_type=MESH)

    for cond, other in (
        (has_left, me - 1),
        (follows, me - 2),
        (relays, me + 2),
        (skipped, me - 3),
    ):
        greet(cond, other)
    targets = (has_right, even & onward, bent, skips)

    @pl.when(has_right)
    def _():
        pl.semaphore_wait(barrier, sum(c.astype(jnp.int32) for c in targets))

    chunk = length // groups

    def remote(src, dst, send, recv, target):
        return pltpu.make_async_remote_copy(
            src_ref=src, dst_ref=dst, send_sem=send, recv_sem=recv,
            device_id={"seq": target}, device_id_type=MESH,
        )

    def rows_of(c):
        return pl.ds(c * chunk, chunk)

    def straight_copy(c, slot, target):
        return remote(
            v_hbm.at[rows_of(c)], val_in.at[slot, rows_of(c)],
            own_send.at[c], val_recv.at[slot, c], target,
        )

    def bent_copy(c):
        return remote(
            v_hbm.at[rows_of(c)], relay_buf.at[rows_of(c)],
            own_send.at[c], relay_recv.at[c], me - 2,
        )

    def relay_copy(c):
        return remote(
            relay_buf.at[rows_of(c)], val_in.at[0, rows_of(c)],
            relay_send.at[c], val_recv.at[0, c], me + 3,
        )

    def pair_copy(src, slot):
        return remote(src, val_in.at[slot], pair_send.at[slot], pair_recv.at[slot], me + 1)

    pairs = [pair_copy(v_hbm, 0), pair_copy(val_in.at[0], 1), pair_copy(val_in.at[1], 2)]
    skip = remote(v_hbm, val_in.at[2], skip_sems.at[0], skip_sems.at[1], me + 3)

    def relay_on(c):
        @pl.when(relays)
        def _():
            bent_copy(c).wait_recv()
            relay_copy(c).start()

    def far_copy(slot, p):
        part = pl.ds(p * sub, sub)
        return pltpu.make_async_remote_copy(
            src_ref=far_out.at[slot, part], dst_ref=far_in.at[slot, part],
            send_sem=far_send.at[slot, p], recv_sem=far_recv.at[slot, p],
            device_id={"seq": me + 1}, device_id_type=MESH,
        )

    ratio = group // sub

    def far_start(slot, g):
        @pl.when(has_right)
        def _():
            for i in range(ratio):
                far_copy(slot, g * ratio + i).start()

    def far_wait(slot, p):
        @pl.when(has_left)
        def _():
            far_copy(slot, p).wait_recv()

    @pl.when(odd & near_side & onward)
    def _():
        for c in range(groups):
            straight_copy(c, 0, me + 1).start()

    @pl.when(even & onward)
    def _():
        for c in range(groups):
            straight_copy(c, 1, me + 2).start()

    @pl.when(bent)
    def _():
        for c in range(groups):
            bent_copy(c).start()

    @pl.when(skips)
    def _():
        skip.start()

    @pl.when(even)
    def _():
        pairs[0].start()

    loads[2].start()
    loads[3].start()

    @pl.when(me == 0)
    def _():
        far_in[...] = jnp.zeros_like(far_in)
        val_in[0] = jnp.zeros_like(val_in[0])
        val_in[1] = jnp.zeros_like(val_in[1])

    @pl.when(even & (chip < 2))
    def _():
        val_in[2] = jnp.zeros_like(val_in[2])

    rows = lax.broadcasted_iota(jnp.int32, (length, length), 0)
    lanes = lax.broadcasted_iota(jnp.int32, (length, length), 1)
    eye_f = (rows == lanes).astype(F32)
    eye_b = eye_f.astype(BF16)
    beta_rows[...] = beta_ref[...].astype(F32)

    seg_own = seg_ref[pl.ds(me, 1), :].astype(F32)
    seg_col = jnp.sum(jnp.where(rows == lanes, seg_own, 0.0), axis=1, keepdims=True)
    bias[0] = jnp.where((seg_own == seg_col) & (lanes <= rows), 0.0, -1e30)
    for r in range(1, depth + 1):
        seg_far = seg_ref[pl.ds(jnp.maximum(me - r, 0), 1), :].astype(F32)
        seen = jnp.where(visit_ref[0, r - 1] > 0, 0.0, -1e30) + jnp.where(me >= r, 0.0, -1e30)
        bias[r] = jnp.where(seg_far == seg_col, 0.0, -1e30) + seen

    def cols(h):
        return pl.ds(pl.multiple_of(h * width, width), width)

    def heads_of(g):
        return [g * group + i for i in range(group)]

    def prepare(g, carry):
        hs = heads_of(g)
        diag = rows == lanes
        ws = [w_ref[:, cols(h)] for h in hs]
        ks = [k_ref[:, cols(h)] for h in hs]
        grams = [nt(w, w) for w in ws]
        crosses = [nt(k, w) for k, w in zip(ks, ws)]
        rns = [
            1.0 / jnp.sqrt(jnp.sum(jnp.where(diag, m, 0.0), axis=0, keepdims=True) + EPSILON)
            for m in grams
        ]
        arows = [beta_rows[pl.ds(h, 1), :] * rn for h, rn in zip(hs, rns)]
        acols = [jnp.sum(jnp.where(diag, a, 0.0), axis=1, keepdims=True) for a in arows]
        lows = [
            jnp.where(rows > lanes, m * a * rn, 0.0) for m, a, rn in zip(grams, acols, rns)
        ]
        apart = rows ^ lanes
        xs = [eye_f - jnp.where(apart == 1, n, 0.0) for n in lows]
        step = 2
        while step < length:
            here = (apart >= step) & (apart < 2 * step)
            halves = [x.astype(BF16) for x in xs]
            lefts = [
                nn(x, jnp.where(here, n, 0.0).astype(BF16)) for x, n in zip(halves, lows)
            ]
            xs = [x - nn(y.astype(BF16), xb) for x, y, xb in zip(xs, lefts, halves)]
            step = step * 2
        halves = [x.astype(BF16) for x in xs]
        pairs = [split(n) for n in lows]
        rests = [
            (eye_f - xb.astype(F32)) - nn(wide(hi, lo), tall(xb, xb))
            for xb, (hi, lo) in zip(halves, pairs)
        ]
        fulls = [xb.astype(F32) + nn(xb, r.astype(BF16)) for xb, r in zip(halves, rests)]
        ms = [split(x * a) for x, a in zip(fulls, arows)]
        bs = [nn(wide(hi, lo), tall(w, w)) for (hi, lo), w in zip(ms, ws)]
        k2 = [split(jnp.where(lanes > rows, c, 0.0)) for c in crosses]
        cs = [
            nt(wide(chi, clo), wide(hi, hi)) + nt(chi, lo)
            for (chi, clo), (hi, lo) in zip(k2, ms)
        ]
        ds = [split(c * rn) for c, rn in zip(cs, rns)]
        moved = [
            k.astype(F32) - nn(wide(hi, lo), tall(w, w))
            for k, (hi, lo), w in zip(ks, ds, ws)
        ]
        for h, b, c, rn, m in zip(hs, bs, cs, rns, moved):
            far_out[0, h] = m.astype(BF16)
            back[h] = wide(*split(b))
            coef[h] = c
            rnorm[pl.ds(h, 1), :] = rn
        far_start(0, g)

        @pl.when(g >= 1)
        def _():
            relay_on(g - 1)

        return carry

    def advance(slot, g):
        hs = heads_of(g)
        for i in range(ratio):
            far_wait(slot, g * ratio + i)
        fs = [far_in[slot, h] for h in hs]
        inner = [nt(wide(f, f), back[h]) * rnorm[pl.ds(h, 1), :] for f, h in zip(fs, hs)]
        new = [
            f.astype(F32) - nn(y.astype(BF16), w_ref[:, cols(h)])
            for f, y, h in zip(fs, inner, hs)
        ]
        for h, x in zip(hs, new):
            far_out[slot + 1, h] = x.astype(BF16)
        far_start(slot + 1, g)

    def query(g):
        hs = heads_of(g)
        qs = [q_ref[:, cols(h)] for h in hs]
        gs = [
            split(jnp.where(lanes <= rows, nt(q, w_ref[:, cols(h)]) * rnorm[pl.ds(h, 1), :], 0.0))
            for q, h in zip(qs, hs)
        ]
        base = [nt(q, k_ref[:, cols(h)]) for q, h in zip(qs, hs)]
        for h, q, (hi, lo), s in zip(hs, qs, gs, base):
            b = back[h]
            bhi, blo = b[:, :width], b[:, width:]
            t = q.astype(F32) - (nn(wide(hi, lo), tall(bhi, bhi)) + nn(hi, blo))
            turned[h] = wide(*split(t * scale))
            chi, clo = split(coef[h])
            o = s - (nt(wide(hi, lo), wide(chi, chi)) + nt(hi, clo))
            own[h] = o * scale + bias[0]

    loads[0].wait()
    loads[1].wait()
    lax.fori_loop(0, groups, prepare, 0)

    relay_on(groups - 1)

    def hop(g, carry):
        advance(0, g)
        return carry

    lax.fori_loop(0, groups, hop, 0)

    def hop_and_query(g, carry):
        query(g)
        advance(1, g)
        return carry

    @pl.when(even & has_left)
    def _():
        for slot in range(2):
            for c in range(groups):
                straight_copy(c, slot, me).wait_recv()

    @pl.when(even)
    def _():
        pairs[1].start()
        pairs[2].start()

    loads[2].wait()
    lax.fori_loop(0, groups, hop_and_query, 0)
    loads[3].wait()

    @pl.when(skipped)
    def _():
        skip.wait_recv()

    @pl.when(odd)
    def _():
        for copy in pairs:
            copy.wait_recv()

    def finish(p, carry):
        hs = [p * sub + i for i in range(sub)]
        far_wait(2, p)
        for h in hs:
            t = turned[h]
            parts = [own[h]]
            for r in range(depth):
                f = far_in[r, h]
                parts.append(nt(t, wide(f, f)) + bias[r + 1])
            top = functools.reduce(jnp.maximum, parts)
            top = jnp.max(top, axis=1, keepdims=True)
            ws = [jnp.exp(p - top) for p in parts]
            total = jnp.sum(functools.reduce(jnp.add, ws), axis=1, keepdims=True)
            vals = [v_ref[:, cols(h)]] + [val_in[r, :, cols(h)] for r in range(depth)]
            mixed = nn(wide(*[x.astype(BF16) for x in ws]), tall(*vals))
            out_ref[:, cols(h)] = (mixed / total).astype(BF16)
        return carry

    lax.fori_loop(0, heads // sub, finish, 0)

    @pl.when(has_right)
    def _():
        for slot in range(depth):
            for p in range(heads // sub):
                far_copy(slot, p).wait_send()

    @pl.when(onward)
    def _():
        for c in range(groups):
            bent_copy(c).wait_send()

    @pl.when(relays)
    def _():
        for c in range(groups):
            relay_copy(c).wait_send()

    @pl.when(skips)
    def _():
        skip.wait_send()

    @pl.when(even)
    def _():
        for copy in pairs:
            copy.wait_send()


def solution(mesh):
    blocks = mesh.shape["seq"]

    def shards(queries, keys, values, transitions, betas, segments, visits):
        length, total = queries.shape
        heads = betas.shape[1]
        width = total // heads
        depth = visits.shape[1]
        group = 4 if heads % 4 == 0 else 1
        sub = 2 if group % 2 == 0 else 1
        parts = heads // sub
        groups = heads // group
        anywhere = pl.BlockSpec(memory_space=pl.ANY)
        whole = pl.BlockSpec(memory_space=pltpu.VMEM)
        return pl.pallas_call(
            functools.partial(kernel, blocks, heads, group, sub),
            out_shape=pltpu.VMEM((length, total), BF16),
            in_specs=[anywhere] * 4 + [whole] * 2 + [pl.BlockSpec(memory_space=pltpu.SMEM)],
            out_specs=whole,
            scratch_shapes=[pltpu.VMEM((length, total), BF16)] * 4 + [
                pltpu.VMEM((depth, heads, length, width), BF16),
                pltpu.VMEM((depth, heads, length, width), BF16),
                pltpu.VMEM((depth, length, total), BF16),
                pltpu.VMEM((length, total), BF16),
                pltpu.VMEM((heads, length, 2 * width), BF16),
                pltpu.VMEM((heads, length, length), F32),
                pltpu.VMEM((heads, length), F32),
                pltpu.VMEM((heads, length), F32),
                pltpu.VMEM((heads, length, 2 * width), BF16),
                pltpu.VMEM((heads, length, length), F32),
                pltpu.VMEM((depth + 1, length, length), F32),
                pltpu.SemaphoreType.DMA((depth, parts)),
                pltpu.SemaphoreType.DMA((depth, parts)),
                pltpu.SemaphoreType.DMA((groups,)),
                pltpu.SemaphoreType.DMA((depth, groups)),
                pltpu.SemaphoreType.DMA((groups,)),
                pltpu.SemaphoreType.DMA((groups,)),
                pltpu.SemaphoreType.DMA((depth,)),
                pltpu.SemaphoreType.DMA((depth,)),
                pltpu.SemaphoreType.DMA((2,)),
                pltpu.SemaphoreType.DMA((4,)),
            ],
            compiler_params=pltpu.CompilerParams(collective_id=0, has_side_effects=True),
        )(
            queries, keys, values, transitions, betas.T,
            segments.reshape(-1, length), visits,
        )

    return jax.shard_map(
        shards,
        mesh=mesh,
        in_specs=(
            P("seq", "head"),
            P("seq", "head"),
            P("seq", "head"),
            P("seq", "head"),
            P("seq", "head"),
            P(),
            P("seq", None),
        ),
        out_specs=P("seq", "head"),
        check_vma=False,
    )
```

```python
import functools

import jax
import jax.numpy as jnp
from jax import lax
from jax.experimental import pallas as pl
from jax.experimental.pallas import tpu as pltpu
from jax.sharding import PartitionSpec as P

EPSILON = 1e-06
MESH = pl.DeviceIdType.MESH
F32 = jnp.float32
BF16 = jnp.bfloat16


def nn(a, b):
    return lax.dot_general(a, b, (((1,), (0,)), ((), ())), preferred_element_type=F32)


def nt(a, b):
    return lax.dot_general(a, b, (((1,), (1,)), ((), ())), preferred_element_type=F32)


def split(x):
    hi = x.astype(BF16)
    return hi, (x - hi.astype(F32)).astype(BF16)


def wide(*parts):
    return jnp.concatenate(parts, axis=1)


def tall(*parts):
    return jnp.concatenate(parts, axis=0)


def kernel(
    blocks, heads, group, sub, q_hbm, k_hbm, v_hbm, w_hbm, beta_hbm, seg_hbm, visit_hbm, out_ref,
    q_ref, k_ref, v_ref, w_ref, beta_ref, seg_ref, visit_ref,
    far_in, far_out, val_in, relay_buf, hub_buf, back, coef, rnorm, beta_rows, turned, own, tops, sums, bias,
    far_send, far_recv, own_send, val_recv, relay_send, relay_recv, hub_send, hub_recv,
    pair_send, pair_recv, skip_sems, load_sem, small_sem,
):
    length = q_ref.shape[0]
    width = q_ref.shape[1] // heads
    depth = far_in.shape[0]
    groups = heads // group
    scale = width ** (-0.5)
    me = lax.axis_index("seq")
    odd = lax.rem(me, 2) == 1
    even = lax.rem(me, 2) == 0
    chip = lax.div(me, 2)
    chips = blocks // 2
    near_side = lax.rem(chip, 2) == 0
    far_side = lax.rem(chip, 2) == 1
    has_left = me >= 1
    has_right = me + 1 < blocks
    onward = chip + 1 < chips
    bent = odd & far_side & onward
    skips = odd & (chip + 2 < chips)
    relays = skips & near_side
    detour = even & far_side & onward
    rejoined = even & near_side & (chip >= 2)
    follows = even & (chip >= 1)
    skipped = even & (chip >= 2)

    barrier = pltpu.get_barrier_semaphore()

    def greet(cond, other):
        @pl.when(cond)
        def _():
            pl.semaphore_signal(barrier, inc=1, device_id={"seq": other}, device_id_type=MESH)

    turns = range(1, chips - 1, 2)
    for c in turns:
        greet(me == 0, 2 * c)
    for cond, other in (
        (has_left, me - 1),
        (follows, me - 2),
        (relays, me + 2),
        (skipped, me - 3),
        (rejoined, 0),
    ):
        greet(cond, other)
    loads = [
        pltpu.make_async_copy(src, dst, load_sem.at[i])
        for i, (src, dst) in enumerate(
            ((w_hbm, w_ref), (k_hbm, k_ref), (q_hbm, q_ref), (v_hbm, v_ref))
        )
    ]
    loads[0].start()
    loads[1].start()
    smalls = [
        pltpu.make_async_copy(src, dst, small_sem.at[i])
        for i, (src, dst) in enumerate(
            ((beta_hbm, beta_ref), (seg_hbm, seg_ref), (visit_hbm, visit_ref))
        )
    ]
    for copy in smalls:
        copy.start()

    targets = (has_right, even & onward, bent, skips, detour) + (me == 0,) * len(turns)

    @pl.when(has_right)
    def _():
        pl.semaphore_wait(barrier, sum(c.astype(jnp.int32) for c in targets))

    chunk = length // groups

    def remote(src, dst, send, recv, target):
        return pltpu.make_async_remote_copy(
            src_ref=src, dst_ref=dst, send_sem=send, recv_sem=recv,
            device_id={"seq": target}, device_id_type=MESH,
        )

    def rows_of(c):
        return pl.ds(c * chunk, chunk)

    def straight_copy(c, slot, target):
        return remote(
            v_hbm.at[rows_of(c)], val_in.at[slot, rows_of(c)],
            own_send.at[c], val_recv.at[slot, c], target,
        )

    def bent_copy(c):
        return remote(
            v_hbm.at[rows_of(c)], relay_buf.at[rows_of(c)],
            own_send.at[c], relay_recv.at[c], me - 2,
        )

    def relay_copy(c):
        return remote(
            relay_buf.at[rows_of(c)], val_in.at[0, rows_of(c)],
            relay_send.at[c], val_recv.at[0, c], me + 3,
        )

    def pair_copy(src, slot):
        return remote(src, val_in.at[slot], pair_send.at[slot], pair_recv.at[slot], me + 1)

    pairs = [pair_copy(v_hbm, 0), pair_copy(val_in.at[0], 1), pair_copy(val_in.at[1], 2)]
    skip = remote(v_hbm, val_in.at[2], skip_sems.at[0], skip_sems.at[1], me + 3)

    final = groups - 1

    def detour_copy(i):
        return remote(
            v_hbm.at[rows_of(final)], hub_buf.at[i],
            own_send.at[final], hub_recv.at[i], 0,
        )

    def rejoin_copy(i, c):
        return remote(
            hub_buf.at[i], val_in.at[1, rows_of(final)],
            hub_send.at[i], val_recv.at[1, final], 2 * c + 2,
        )

    def relay_on(c):
        @pl.when(relays)
        def _():
            bent_copy(c).wait_recv()
            relay_copy(c).start()

    def far_copy(slot, p):
        part = pl.ds(p * sub, sub)
        return pltpu.make_async_remote_copy(
            src_ref=far_out.at[slot, part], dst_ref=far_in.at[slot, part],
            send_sem=far_send.at[slot, p], recv_sem=far_recv.at[slot, p],
            device_id={"seq": me + 1}, device_id_type=MESH,
        )

    ratio = group // sub

    def far_start(slot, g):
        @pl.when(has_right)
        def _():
            for i in range(ratio):
                far_copy(slot, g * ratio + i).start()

    def far_wait(slot, p):
        @pl.when(has_left)
        def _():
            far_copy(slot, p).wait_recv()

    @pl.when(odd & near_side & onward)
    def _():
        for c in range(groups):
            straight_copy(c, 0, me + 1).start()

    @pl.when(detour)
    def _():
        detour_copy(lax.div(chip, 2)).start()

    @pl.when(even & onward)
    def _():
        for c in range(final):
            straight_copy(c, 1, me + 2).start()

    @pl.when(even & near_side & onward)
    def _():
        straight_copy(final, 1, me + 2).start()

    @pl.when(bent)
    def _():
        for c in range(groups):
            bent_copy(c).start()

    @pl.when(skips)
    def _():
        skip.start()

    @pl.when(even)
    def _():
        pairs[0].start()

    loads[2].start()
    loads[3].start()

    @pl.when(me == 0)
    def _():
        far_in[...] = jnp.zeros_like(far_in)
        val_in[0] = jnp.zeros_like(val_in[0])
        val_in[1] = jnp.zeros_like(val_in[1])

    @pl.when(even & (chip < 2))
    def _():
        val_in[2] = jnp.zeros_like(val_in[2])

    rows = lax.broadcasted_iota(jnp.int32, (length, length), 0)
    lanes = lax.broadcasted_iota(jnp.int32, (length, length), 1)
    eye_f = (rows == lanes).astype(F32)
    eye_b = eye_f.astype(BF16)
    for copy in smalls:
        copy.wait()
    beta_rows[...] = beta_ref[...].astype(F32)

    seg_own = seg_ref[pl.ds(me, 1), :].astype(F32)
    seg_col = jnp.sum(jnp.where(rows == lanes, seg_own, 0.0), axis=1, keepdims=True)
    bias[0] = jnp.where((seg_own == seg_col) & (lanes <= rows), 0.0, -1e30)
    for r in range(1, depth + 1):
        seg_far = seg_ref[pl.ds(jnp.maximum(me - r, 0), 1), :].astype(F32)
        seen = jnp.where(visit_ref[0, r - 1] > 0, 0.0, -1e30) + jnp.where(me >= r, 0.0, -1e30)
        bias[r] = jnp.where(seg_far == seg_col, 0.0, -1e30) + seen

    def cols(h):
        return pl.ds(pl.multiple_of(h * width, width), width)

    def heads_of(g):
        return [g * group + i for i in range(group)]

    def prepare(g, carry):
        hs = heads_of(g)
        diag = rows == lanes
        ws = [w_ref[:, cols(h)] for h in hs]
        ks = [k_ref[:, cols(h)] for h in hs]
        grams = [nt(w, w) for w in ws]
        crosses = [nt(k, w) for k, w in zip(ks, ws)]
        rns = [
            1.0 / jnp.sqrt(jnp.sum(jnp.where(diag, m, 0.0), axis=0, keepdims=True) + EPSILON)
            for m in grams
        ]
        arows = [beta_rows[pl.ds(h, 1), :] * rn for h, rn in zip(hs, rns)]
        acols = [jnp.sum(jnp.where(diag, a, 0.0), axis=1, keepdims=True) for a in arows]
        lows = [
            jnp.where(rows > lanes, m * a * rn, 0.0) for m, a, rn in zip(grams, acols, rns)
        ]
        apart = rows ^ lanes
        xs = [eye_f - jnp.where(apart == 1, n, 0.0) for n in lows]
        step = 2
        while step < length:
            here = (apart >= step) & (apart < 2 * step)
            halves = [x.astype(BF16) for x in xs]
            lefts = [
                nn(x, jnp.where(here, n, 0.0).astype(BF16)) for x, n in zip(halves, lows)
            ]
            xs = [x - nn(y.astype(BF16), xb) for x, y, xb in zip(xs, lefts, halves)]
            step = step * 2
        halves = [x.astype(BF16) for x in xs]
        pairs = [split(n) for n in lows]
        rests = [
            (eye_f - xb.astype(F32)) - nn(wide(hi, lo), tall(xb, xb))
            for xb, (hi, lo) in zip(halves, pairs)
        ]
        fulls = [xb.astype(F32) + nn(xb, r.astype(BF16)) for xb, r in zip(halves, rests)]
        ms = [split(x * a) for x, a in zip(fulls, arows)]
        bs = [nn(wide(hi, lo), tall(w, w)) for (hi, lo), w in zip(ms, ws)]
        k2 = [split(jnp.where(lanes > rows, c, 0.0)) for c in crosses]
        cs = [
            nt(wide(chi, clo), wide(hi, hi)) + nt(chi, lo)
            for (chi, clo), (hi, lo) in zip(k2, ms)
        ]
        ds = [split(c * rn) for c, rn in zip(cs, rns)]
        moved = [
            k.astype(F32) - nn(wide(hi, lo), tall(w, w))
            for k, (hi, lo), w in zip(ks, ds, ws)
        ]
        for h, b, c, rn, m in zip(hs, bs, cs, rns, moved):
            far_out[0, h] = m.astype(BF16)
            back[h] = wide(*split(b))
            coef[h] = c
            rnorm[pl.ds(h, 1), :] = rn
        far_start(0, g)

        @pl.when(g >= 1)
        def _():
            relay_on(g - 1)

        @pl.when((me == 0) & (g == groups // 2))
        def _():
            for i, c in reversed(list(enumerate(turns))):
                detour_copy(i).wait_recv()
                rejoin_copy(i, c).start()

        return carry

    def advance(slot, g):
        hs = heads_of(g)
        for i in range(ratio):
            far_wait(slot, g * ratio + i)
        fs = [far_in[slot, h] for h in hs]
        inner = [nt(wide(f, f), back[h]) * rnorm[pl.ds(h, 1), :] for f, h in zip(fs, hs)]
        new = [
            f.astype(F32) - nn(y.astype(BF16), w_ref[:, cols(h)])
            for f, y, h in zip(fs, inner, hs)
        ]
        for h, x in zip(hs, new):
            far_out[slot + 1, h] = x.astype(BF16)
        far_start(slot + 1, g)

    def query(g):
        hs = heads_of(g)
        qs = [q_ref[:, cols(h)] for h in hs]
        gs = [
            split(jnp.where(lanes <= rows, nt(q, w_ref[:, cols(h)]) * rnorm[pl.ds(h, 1), :], 0.0))
            for q, h in zip(qs, hs)
        ]
        base = [nt(q, k_ref[:, cols(h)]) for q, h in zip(qs, hs)]
        for h, q, (hi, lo), s in zip(hs, qs, gs, base):
            b = back[h]
            bhi, blo = b[:, :width], b[:, width:]
            t = q.astype(F32) - (nn(wide(hi, lo), tall(bhi, bhi)) + nn(hi, blo))
            turned[h] = wide(*split(t * scale))
            chi, clo = split(coef[h])
            o = s - (nt(wide(hi, lo), wide(chi, chi)) + nt(hi, clo))
            own[h] = o * scale + bias[0]

    loads[0].wait()
    loads[1].wait()
    lax.fori_loop(0, groups, prepare, 0)

    relay_on(groups - 1)


    def start(g):
        near = depth - 1
        for h in heads_of(g):
            t = turned[h]
            parts = [own[h]]
            for r in range(near):
                f = far_in[r, h]
                parts.append(nt(t, wide(f, f)) + bias[r + 1])
            top = jnp.max(functools.reduce(jnp.maximum, parts), axis=1, keepdims=True)
            ws = [jnp.exp(p - top) for p in parts]
            total = jnp.sum(functools.reduce(jnp.add, ws), axis=1, keepdims=True)
            tops[h] = jnp.broadcast_to(top, (length, width))
            sums[h] = jnp.broadcast_to(total, (length, width))
            vals = [v_ref[:, cols(h)]] + [val_in[r, :, cols(h)] for r in range(near)]
            own[h] = nn(wide(*[x.astype(BF16) for x in ws]), tall(*vals))

    def share_values():
        @pl.when(even & has_left)
        def _():
            for slot in range(2):
                for c in range(groups):
                    straight_copy(c, slot, me).wait_recv()

        @pl.when(even)
        def _():
            pairs[1].start()
            pairs[2].start()

    def first_hop(g, carry):
        query(g)
        advance(0, g)

        @pl.when(g == groups // 2)
        def _():
            share_values()

        return carry

    def second_hop(g, carry):
        advance(1, g)
        start(g)
        return carry

    loads[2].wait()
    lax.fori_loop(0, groups, first_hop, 0)
    loads[3].wait()

    @pl.when(odd)
    def _():
        pairs[0].wait_recv()
        pairs[1].wait_recv()

    lax.fori_loop(0, groups, second_hop, 0)

    @pl.when(skipped)
    def _():
        skip.wait_recv()

    @pl.when(odd)
    def _():
        pairs[2].wait_recv()

    def finish(hs):
        last = depth - 1
        fs = [far_in[last, h] for h in hs]
        ss = [nt(turned[h], wide(f, f)) + bias[depth] for h, f in zip(hs, fs)]
        olds = [tops[h] for h in hs]
        news = [
            jnp.maximum(old, jnp.max(s, axis=1, keepdims=True)) for old, s in zip(olds, ss)
        ]
        ws = [jnp.exp(s - top) for s, top in zip(ss, news)]
        keeps = [jnp.exp(old - top) for old, top in zip(olds, news)]
        adds = [nn(w.astype(BF16), val_in[last, :, cols(h)]) for w, h in zip(ws, hs)]
        for h, w, keep, add in zip(hs, ws, keeps, adds):
            total = sums[h] * keep + jnp.sum(w, axis=1, keepdims=True)
            out_ref[:, cols(h)] = ((own[h] * keep + add) / total).astype(BF16)

    def finish_group(g, carry):
        for i in range(ratio):
            far_wait(depth - 1, g * ratio + i)
        finish(heads_of(g))
        return carry

    def finish_part(p, carry):
        far_wait(depth - 1, p)
        finish([p * sub + i for i in range(sub)])
        return carry

    lax.fori_loop(0, groups - 1, finish_group, 0)
    lax.fori_loop((groups - 1) * ratio, groups * ratio, finish_part, 0)

    @pl.when(has_right)
    def _():
        for slot in range(depth):
            for p in range(heads // sub):
                far_copy(slot, p).wait_send()

    @pl.when(onward)
    def _():
        for c in range(groups):
            bent_copy(c).wait_send()

    @pl.when(relays)
    def _():
        for c in range(groups):
            relay_copy(c).wait_send()

    @pl.when(me == 0)
    def _():
        for i, c in enumerate(turns):
            rejoin_copy(i, c).wait_send()

    @pl.when(skips)
    def _():
        skip.wait_send()

    @pl.when(even)
    def _():
        for copy in pairs:
            copy.wait_send()


def solution(mesh):
    blocks = mesh.shape["seq"]

    def shards(queries, keys, values, transitions, betas, segments, visits):
        length, total = queries.shape
        heads = betas.shape[1]
        width = total // heads
        depth = visits.shape[1]
        group = 4 if heads % 4 == 0 else 1
        sub = 2 if group % 2 == 0 else 1
        parts = heads // sub
        groups = heads // group
        turns = max(1, len(range(1, blocks // 2 - 1, 2)))
        anywhere = pl.BlockSpec(memory_space=pl.ANY)
        whole = pl.BlockSpec(memory_space=pltpu.VMEM)
        return pl.pallas_call(
            functools.partial(kernel, blocks, heads, group, sub),
            out_shape=pltpu.VMEM((length, total), BF16),
            in_specs=[anywhere] * 7,
            out_specs=whole,
            scratch_shapes=[pltpu.VMEM((length, total), BF16)] * 4 + [
                pltpu.VMEM((heads, length), BF16),
                pltpu.VMEM((blocks, length), jnp.int32),
                pltpu.SMEM((1, depth), jnp.int32),
                pltpu.VMEM((depth, heads, length, width), BF16),
                pltpu.VMEM((depth, heads, length, width), BF16),
                pltpu.VMEM((depth, length, total), BF16),
                pltpu.VMEM((length, total), BF16),
                pltpu.VMEM((turns, length // groups, total), BF16),
                pltpu.VMEM((heads, length, 2 * width), BF16),
                pltpu.VMEM((heads, length, length), F32),
                pltpu.VMEM((heads, length), F32),
                pltpu.VMEM((heads, length), F32),
                pltpu.VMEM((heads, length, 2 * width), BF16),
                pltpu.VMEM((heads, length, length), F32),
                pltpu.VMEM((heads, length, width), F32),
                pltpu.VMEM((heads, length, width), F32),
                pltpu.VMEM((depth + 1, length, length), F32),
                pltpu.SemaphoreType.DMA((depth, parts)),
                pltpu.SemaphoreType.DMA((depth, parts)),
                pltpu.SemaphoreType.DMA((groups,)),
                pltpu.SemaphoreType.DMA((depth, groups)),
                pltpu.SemaphoreType.DMA((groups,)),
                pltpu.SemaphoreType.DMA((groups,)),
                pltpu.SemaphoreType.DMA((turns,)),
                pltpu.SemaphoreType.DMA((turns,)),
                pltpu.SemaphoreType.DMA((depth,)),
                pltpu.SemaphoreType.DMA((depth,)),
                pltpu.SemaphoreType.DMA((2,)),
                pltpu.SemaphoreType.DMA((4,)),
                pltpu.SemaphoreType.DMA((3,)),
            ],
            compiler_params=pltpu.CompilerParams(collective_id=0, has_side_effects=True),
        )(
            queries, keys, values, transitions, betas.T,
            segments.reshape(-1, length), visits,
        )

    return jax.shard_map(
        shards,
        mesh=mesh,
        in_specs=(
            P("seq", "head"),
            P("seq", "head"),
            P("seq", "head"),
            P("seq", "head"),
            P("seq", "head"),
            P(),
            P("seq", None),
        ),
        out_specs=P("seq", "head"),
        check_vma=False,
    )
```

```python
import functools

import jax
import jax.numpy as jnp
from jax import lax
from jax.experimental import pallas as pl
from jax.experimental.pallas import tpu as pltpu
from jax.sharding import PartitionSpec as P

EPSILON = 1e-06
MESH = pl.DeviceIdType.MESH
F32 = jnp.float32
BF16 = jnp.bfloat16


def nn(a, b):
    return lax.dot_general(a, b, (((1,), (0,)), ((), ())), preferred_element_type=F32)


def nt(a, b):
    return lax.dot_general(a, b, (((1,), (1,)), ((), ())), preferred_element_type=F32)


def split(x):
    hi = x.astype(BF16)
    return hi, (x - hi.astype(F32)).astype(BF16)


def wide(*parts):
    return jnp.concatenate(parts, axis=1)


def tall(*parts):
    return jnp.concatenate(parts, axis=0)


def kernel(
    blocks, heads, group, sub, q_hbm, k_hbm, v_hbm, w_hbm, beta_hbm, seg_hbm, visit_hbm, out_ref,
    q_ref, k_ref, v_ref, w_ref, beta_ref, seg_ref, visit_ref,
    far_in, far_out, val_in, relay_buf, hub_buf, back, coef, rnorm, beta_rows, turned, own, tops, sums, bias,
    far_send, far_recv, own_send, val_recv, relay_send, relay_recv, hub_send, hub_recv,
    pair_send, pair_recv, skip_sems, load_sem, small_sem,
):
    length = q_ref.shape[0]
    width = q_ref.shape[1] // heads
    depth = far_in.shape[0]
    groups = heads // group
    scale = width ** (-0.5)
    me = lax.axis_index("seq")
    odd = lax.rem(me, 2) == 1
    even = lax.rem(me, 2) == 0
    chip = lax.div(me, 2)
    chips = blocks // 2
    near_side = lax.rem(chip, 2) == 0
    far_side = lax.rem(chip, 2) == 1
    has_left = me >= 1
    has_right = me + 1 < blocks
    onward = chip + 1 < chips
    bent = odd & far_side & onward
    skips = odd & (chip + 2 < chips)
    relays = skips & near_side
    detour = even & far_side & onward
    rejoined = even & near_side & (chip >= 2)
    follows = even & (chip >= 1)
    skipped = even & (chip >= 2)

    barrier = pltpu.get_barrier_semaphore()

    def greet(cond, other):
        @pl.when(cond)
        def _():
            pl.semaphore_signal(barrier, inc=1, device_id={"seq": other}, device_id_type=MESH)

    turns = range(1, chips - 1, 2)
    for c in turns:
        greet(me == 0, 2 * c)
    for cond, other in (
        (has_left, me - 1),
        (follows, me - 2),
        (relays, me + 2),
        (skipped, me - 3),
        (rejoined, 0),
    ):
        greet(cond, other)
    loads = [
        pltpu.make_async_copy(src, dst, load_sem.at[i])
        for i, (src, dst) in enumerate(
            ((w_hbm, w_ref), (k_hbm, k_ref), (q_hbm, q_ref), (v_hbm, v_ref))
        )
    ]
    loads[0].start()
    loads[1].start()
    smalls = [
        pltpu.make_async_copy(src, dst, small_sem.at[i])
        for i, (src, dst) in enumerate(
            ((beta_hbm, beta_ref), (seg_hbm, seg_ref), (visit_hbm, visit_ref))
        )
    ]
    for copy in smalls:
        copy.start()

    targets = (has_right, even & onward, bent, skips, detour) + (me == 0,) * len(turns)

    @pl.when(has_right)
    def _():
        pl.semaphore_wait(barrier, sum(c.astype(jnp.int32) for c in targets))

    chunk = length // groups

    def remote(src, dst, send, recv, target):
        return pltpu.make_async_remote_copy(
            src_ref=src, dst_ref=dst, send_sem=send, recv_sem=recv,
            device_id={"seq": target}, device_id_type=MESH,
        )

    def rows_of(c):
        return pl.ds(c * chunk, chunk)

    def straight_copy(c, slot, target):
        return remote(
            v_hbm.at[rows_of(c)], val_in.at[slot, rows_of(c)],
            own_send.at[c], val_recv.at[slot, c], target,
        )

    def bent_copy(c):
        return remote(
            v_hbm.at[rows_of(c)], relay_buf.at[rows_of(c)],
            own_send.at[c], relay_recv.at[c], me - 2,
        )

    def relay_copy(c):
        return remote(
            relay_buf.at[rows_of(c)], val_in.at[0, rows_of(c)],
            relay_send.at[c], val_recv.at[0, c], me + 3,
        )

    def pair_copy(src, slot):
        return remote(src, val_in.at[slot], pair_send.at[slot], pair_recv.at[slot], me + 1)

    pairs = [pair_copy(v_hbm, 0), pair_copy(val_in.at[0], 1), pair_copy(val_in.at[1], 2)]
    skip = remote(v_hbm, val_in.at[2], skip_sems.at[0], skip_sems.at[1], me + 3)

    final = groups - 1

    def detour_copy(i):
        return remote(
            v_hbm.at[rows_of(final)], hub_buf.at[i],
            own_send.at[final], hub_recv.at[i], 0,
        )

    def rejoin_copy(i, c):
        return remote(
            hub_buf.at[i], val_in.at[1, rows_of(final)],
            hub_send.at[i], val_recv.at[1, final], 2 * c + 2,
        )

    def relay_on(c):
        @pl.when(relays)
        def _():
            bent_copy(c).wait_recv()
            relay_copy(c).start()

    def far_copy(slot, p):
        part = pl.ds(p * sub, sub)
        return pltpu.make_async_remote_copy(
            src_ref=far_out.at[slot, part], dst_ref=far_in.at[slot, part],
            send_sem=far_send.at[slot, p], recv_sem=far_recv.at[slot, p],
            device_id={"seq": me + 1}, device_id_type=MESH,
        )

    ratio = group // sub

    def far_start(slot, g):
        @pl.when(has_right)
        def _():
            for i in range(ratio):
                far_copy(slot, g * ratio + i).start()

    def far_wait(slot, p):
        @pl.when(has_left)
        def _():
            far_copy(slot, p).wait_recv()

    @pl.when(odd & near_side & onward)
    def _():
        for c in range(groups):
            straight_copy(c, 0, me + 1).start()

    @pl.when(detour)
    def _():
        detour_copy(lax.div(chip, 2)).start()

    @pl.when(even & onward)
    def _():
        for c in range(final):
            straight_copy(c, 1, me + 2).start()

    @pl.when(even & near_side & onward)
    def _():
        straight_copy(final, 1, me + 2).start()

    @pl.when(bent)
    def _():
        for c in range(groups):
            bent_copy(c).start()

    @pl.when(skips)
    def _():
        skip.start()

    @pl.when(even)
    def _():
        pairs[0].start()

    loads[2].start()
    loads[3].start()

    @pl.when(me == 0)
    def _():
        far_in[...] = jnp.zeros_like(far_in)
        val_in[0] = jnp.zeros_like(val_in[0])
        val_in[1] = jnp.zeros_like(val_in[1])

    @pl.when(even & (chip < 2))
    def _():
        val_in[2] = jnp.zeros_like(val_in[2])

    rows = lax.broadcasted_iota(jnp.int32, (length, length), 0)
    lanes = lax.broadcasted_iota(jnp.int32, (length, length), 1)
    eye_f = (rows == lanes).astype(F32)
    eye_b = eye_f.astype(BF16)
    for copy in smalls:
        copy.wait()
    beta_rows[...] = beta_ref[...].astype(F32)

    seg_own = seg_ref[pl.ds(me, 1), :].astype(F32)
    seg_col = jnp.sum(jnp.where(rows == lanes, seg_own, 0.0), axis=1, keepdims=True)
    bias[0] = jnp.where((seg_own == seg_col) & (lanes <= rows), 0.0, -1e30)
    for r in range(1, depth + 1):
        seg_far = seg_ref[pl.ds(jnp.maximum(me - r, 0), 1), :].astype(F32)
        seen = jnp.where(visit_ref[0, r - 1] > 0, 0.0, -1e30) + jnp.where(me >= r, 0.0, -1e30)
        bias[r] = jnp.where(seg_far == seg_col, 0.0, -1e30) + seen

    def cols(h):
        return pl.ds(pl.multiple_of(h * width, width), width)

    def heads_of(g):
        return [g * group + i for i in range(group)]

    def prepare(g, carry):
        hs = heads_of(g)
        diag = rows == lanes
        ws = [w_ref[:, cols(h)] for h in hs]
        ks = [k_ref[:, cols(h)] for h in hs]
        grams = [nt(w, w) for w in ws]
        crosses = [nt(k, w) for k, w in zip(ks, ws)]
        rns = [
            1.0 / jnp.sqrt(jnp.sum(jnp.where(diag, m, 0.0), axis=0, keepdims=True) + EPSILON)
            for m in grams
        ]
        arows = [beta_rows[pl.ds(h, 1), :] * rn for h, rn in zip(hs, rns)]
        acols = [jnp.sum(jnp.where(diag, a, 0.0), axis=1, keepdims=True) for a in arows]
        lows = [
            jnp.where(rows > lanes, m * a * rn, 0.0) for m, a, rn in zip(grams, acols, rns)
        ]
        apart = rows ^ lanes
        xs = [eye_f - jnp.where(apart == 1, n, 0.0) for n in lows]
        step = 2
        while step < length:
            here = (apart >= step) & (apart < 2 * step)
            halves = [x.astype(BF16) for x in xs]
            lefts = [
                nn(x, jnp.where(here, n, 0.0).astype(BF16)) for x, n in zip(halves, lows)
            ]
            xs = [x - nn(y.astype(BF16), xb) for x, y, xb in zip(xs, lefts, halves)]
            step = step * 2
        halves = [x.astype(BF16) for x in xs]
        pairs = [split(n) for n in lows]
        rests = [
            (eye_f - xb.astype(F32)) - nn(wide(hi, lo), tall(xb, xb))
            for xb, (hi, lo) in zip(halves, pairs)
        ]
        fulls = [xb.astype(F32) + nn(xb, r.astype(BF16)) for xb, r in zip(halves, rests)]
        ms = [split(x * a) for x, a in zip(fulls, arows)]
        bs = [nn(wide(hi, lo), tall(w, w)) for (hi, lo), w in zip(ms, ws)]
        k2 = [split(jnp.where(lanes > rows, c, 0.0)) for c in crosses]
        cs = [
            nt(wide(chi, clo), wide(hi, hi)) + nt(chi, lo)
            for (chi, clo), (hi, lo) in zip(k2, ms)
        ]
        ds = [split(c * rn) for c, rn in zip(cs, rns)]
        moved = [
            k.astype(F32) - nn(wide(hi, lo), tall(w, w))
            for k, (hi, lo), w in zip(ks, ds, ws)
        ]
        for h, b, c, rn, m in zip(hs, bs, cs, rns, moved):
            far_out[0, h] = m.astype(BF16)
            back[h] = wide(*split(b))
            coef[h] = c
            rnorm[pl.ds(h, 1), :] = rn
        far_start(0, g)

        @pl.when(g >= groups // 2)
        def _():
            relay_on(g - groups // 2)

        @pl.when((me == 0) & (g == groups // 2))
        def _():
            for i, c in reversed(list(enumerate(turns))):
                detour_copy(i).wait_recv()
                rejoin_copy(i, c).start()

        return carry

    def advance(slot, g):
        hs = heads_of(g)
        for i in range(ratio):
            far_wait(slot, g * ratio + i)
        fs = [far_in[slot, h] for h in hs]
        inner = [nt(wide(f, f), back[h]) * rnorm[pl.ds(h, 1), :] for f, h in zip(fs, hs)]
        new = [
            f.astype(F32) - nn(y.astype(BF16), w_ref[:, cols(h)])
            for f, y, h in zip(fs, inner, hs)
        ]
        for h, x in zip(hs, new):
            far_out[slot + 1, h] = x.astype(BF16)
        far_start(slot + 1, g)

    def query(g):
        hs = heads_of(g)
        qs = [q_ref[:, cols(h)] for h in hs]
        gs = [
            split(jnp.where(lanes <= rows, nt(q, w_ref[:, cols(h)]) * rnorm[pl.ds(h, 1), :], 0.0))
            for q, h in zip(qs, hs)
        ]
        base = [nt(q, k_ref[:, cols(h)]) for q, h in zip(qs, hs)]
        for h, q, (hi, lo), s in zip(hs, qs, gs, base):
            b = back[h]
            bhi, blo = b[:, :width], b[:, width:]
            t = q.astype(F32) - (nn(wide(hi, lo), tall(bhi, bhi)) + nn(hi, blo))
            turned[h] = wide(*split(t * scale))
            chi, clo = split(coef[h])
            o = s - (nt(wide(hi, lo), wide(chi, chi)) + nt(hi, clo))
            own[h] = o * scale + bias[0]

    loads[0].wait()
    loads[1].wait()
    lax.fori_loop(0, groups, prepare, 0)


    def start(g):
        near = depth - 1
        for h in heads_of(g):
            t = turned[h]
            parts = [own[h]]
            for r in range(near):
                f = far_in[r, h]
                parts.append(nt(t, wide(f, f)) + bias[r + 1])
            top = jnp.max(functools.reduce(jnp.maximum, parts), axis=1, keepdims=True)
            ws = [jnp.exp(p - top) for p in parts]
            total = jnp.sum(functools.reduce(jnp.add, ws), axis=1, keepdims=True)
            tops[h] = jnp.broadcast_to(top, (length, width))
            sums[h] = jnp.broadcast_to(total, (length, width))
            vals = [v_ref[:, cols(h)]] + [val_in[r, :, cols(h)] for r in range(near)]
            own[h] = nn(wide(*[x.astype(BF16) for x in ws]), tall(*vals))

    def share_values():
        @pl.when(even & has_left)
        def _():
            for slot in range(2):
                for c in range(groups):
                    straight_copy(c, slot, me).wait_recv()

        @pl.when(even)
        def _():
            pairs[1].start()
            pairs[2].start()

    def first_hop(g, carry):
        query(g)
        advance(0, g)

        @pl.when((g >= 1) & (g <= groups // 2))
        def _():
            relay_on(g - 1 + groups - groups // 2)

        return carry

    def second_hop(g, carry):
        advance(1, g)

        @pl.when(odd & (g == 1))
        def _():
            pairs[0].wait_recv()
            pairs[1].wait_recv()

        @pl.when(g >= 1)
        def _():
            start(g - 1)

        return carry

    loads[2].wait()
    lax.fori_loop(0, groups, first_hop, 0)
    loads[3].wait()
    share_values()
    lax.fori_loop(0, groups, second_hop, 0)
    start(groups - 1)

    @pl.when(skipped)
    def _():
        skip.wait_recv()

    @pl.when(odd)
    def _():
        pairs[2].wait_recv()

    def finish(hs):
        last = depth - 1
        fs = [far_in[last, h] for h in hs]
        ss = [nt(turned[h], wide(f, f)) + bias[depth] for h, f in zip(hs, fs)]
        olds = [tops[h] for h in hs]
        news = [
            jnp.maximum(old, jnp.max(s, axis=1, keepdims=True)) for old, s in zip(olds, ss)
        ]
        ws = [jnp.exp(s - top) for s, top in zip(ss, news)]
        keeps = [jnp.exp(old - top) for old, top in zip(olds, news)]
        adds = [nn(w.astype(BF16), val_in[last, :, cols(h)]) for w, h in zip(ws, hs)]
        for h, w, keep, add in zip(hs, ws, keeps, adds):
            total = sums[h] * keep + jnp.sum(w, axis=1, keepdims=True)
            out_ref[:, cols(h)] = ((own[h] * keep + add) / total).astype(BF16)

    def finish_group(g, carry):
        for i in range(ratio):
            far_wait(depth - 1, g * ratio + i)
        finish(heads_of(g))
        return carry

    def finish_part(p, carry):
        far_wait(depth - 1, p)
        finish([p * sub + i for i in range(sub)])
        return carry

    lax.fori_loop(0, groups - 1, finish_group, 0)
    lax.fori_loop((groups - 1) * ratio, groups * ratio, finish_part, 0)

    @pl.when(has_right)
    def _():
        for slot in range(depth):
            for p in range(heads // sub):
                far_copy(slot, p).wait_send()

    @pl.when(onward)
    def _():
        for c in range(groups):
            bent_copy(c).wait_send()

    @pl.when(relays)
    def _():
        for c in range(groups):
            relay_copy(c).wait_send()

    @pl.when(me == 0)
    def _():
        for i, c in enumerate(turns):
            rejoin_copy(i, c).wait_send()

    @pl.when(skips)
    def _():
        skip.wait_send()

    @pl.when(even)
    def _():
        for copy in pairs:
            copy.wait_send()


def solution(mesh):
    blocks = mesh.shape["seq"]

    def shards(queries, keys, values, transitions, betas, segments, visits):
        length, total = queries.shape
        heads = betas.shape[1]
        width = total // heads
        depth = visits.shape[1]
        group = 4 if heads % 4 == 0 else 1
        sub = 2 if group % 2 == 0 else 1
        parts = heads // sub
        groups = heads // group
        turns = max(1, len(range(1, blocks // 2 - 1, 2)))
        anywhere = pl.BlockSpec(memory_space=pl.ANY)
        whole = pl.BlockSpec(memory_space=pltpu.VMEM)
        return pl.pallas_call(
            functools.partial(kernel, blocks, heads, group, sub),
            out_shape=pltpu.VMEM((length, total), BF16),
            in_specs=[anywhere] * 7,
            out_specs=whole,
            scratch_shapes=[pltpu.VMEM((length, total), BF16)] * 4 + [
                pltpu.VMEM((heads, length), BF16),
                pltpu.VMEM((blocks, length), jnp.int32),
                pltpu.SMEM((1, depth), jnp.int32),
                pltpu.VMEM((depth, heads, length, width), BF16),
                pltpu.VMEM((depth, heads, length, width), BF16),
                pltpu.VMEM((depth, length, total), BF16),
                pltpu.VMEM((length, total), BF16),
                pltpu.VMEM((turns, length // groups, total), BF16),
                pltpu.VMEM((heads, length, 2 * width), BF16),
                pltpu.VMEM((heads, length, length), F32),
                pltpu.VMEM((heads, length), F32),
                pltpu.VMEM((heads, length), F32),
                pltpu.VMEM((heads, length, 2 * width), BF16),
                pltpu.VMEM((heads, length, length), F32),
                pltpu.VMEM((heads, length, width), F32),
                pltpu.VMEM((heads, length, width), F32),
                pltpu.VMEM((depth + 1, length, length), F32),
                pltpu.SemaphoreType.DMA((depth, parts)),
                pltpu.SemaphoreType.DMA((depth, parts)),
                pltpu.SemaphoreType.DMA((groups,)),
                pltpu.SemaphoreType.DMA((depth, groups)),
                pltpu.SemaphoreType.DMA((groups,)),
                pltpu.SemaphoreType.DMA((groups,)),
                pltpu.SemaphoreType.DMA((turns,)),
                pltpu.SemaphoreType.DMA((turns,)),
                pltpu.SemaphoreType.DMA((depth,)),
                pltpu.SemaphoreType.DMA((depth,)),
                pltpu.SemaphoreType.DMA((2,)),
                pltpu.SemaphoreType.DMA((4,)),
                pltpu.SemaphoreType.DMA((3,)),
            ],
            compiler_params=pltpu.CompilerParams(collective_id=0, has_side_effects=True),
        )(
            queries, keys, values, transitions, betas.T,
            segments.reshape(-1, length), visits,
        )

    return jax.shard_map(
        shards,
        mesh=mesh,
        in_specs=(
            P("seq", "head"),
            P("seq", "head"),
            P("seq", "head"),
            P("seq", "head"),
            P("seq", "head"),
            P(),
            P("seq", None),
        ),
        out_specs=P("seq", "head"),
        check_vma=False,
    )
```

```python
import functools

import jax
import jax.numpy as jnp
from jax import lax
from jax.experimental import pallas as pl
from jax.experimental.pallas import tpu as pltpu
from jax.sharding import PartitionSpec as P

EPSILON = 1e-06
MESH = pl.DeviceIdType.MESH
F32 = jnp.float32
BF16 = jnp.bfloat16


def nn(a, b):
    return lax.dot_general(a, b, (((1,), (0,)), ((), ())), preferred_element_type=F32)


def nt(a, b):
    return lax.dot_general(a, b, (((1,), (1,)), ((), ())), preferred_element_type=F32)


def split(x):
    hi = x.astype(BF16)
    return hi, (x - hi.astype(F32)).astype(BF16)


def wide(*parts):
    return jnp.concatenate(parts, axis=1)


def tall(*parts):
    return jnp.concatenate(parts, axis=0)


def kernel(
    blocks, heads, group, sub, q_hbm, k_hbm, v_hbm, w_hbm, beta_hbm, seg_hbm, visit_hbm, out_ref,
    q_ref, k_ref, v_ref, w_ref, beta_ref, seg_ref, visit_ref,
    far_in, far_out, val_in, relay_buf, hub_buf, back, coef, rnorm, beta_rows, turned, own, tops, sums, bias,
    far_send, far_recv, own_send, val_recv, relay_send, relay_recv, hub_send, hub_recv,
    pair_send, pair_recv, skip_sems, load_sem, small_sem, clear_sem,
):
    length = q_ref.shape[0]
    width = q_ref.shape[1] // heads
    depth = far_in.shape[0]
    groups = heads // group
    scale = width ** (-0.5)
    me = lax.axis_index("seq")
    odd = lax.rem(me, 2) == 1
    even = lax.rem(me, 2) == 0
    chip = lax.div(me, 2)
    chips = blocks // 2
    near_side = lax.rem(chip, 2) == 0
    far_side = lax.rem(chip, 2) == 1
    has_left = me >= 1
    has_right = me + 1 < blocks
    onward = chip + 1 < chips
    bent = odd & far_side & onward
    skips = odd & (chip + 2 < chips)
    relays = skips & near_side
    detour = even & far_side & onward
    clears = bent & (chip >= 3)
    held = far_side & (chip + 3 < chips)
    late = min(1, groups - 1)
    rejoined = even & near_side & (chip >= 2)
    follows = even & (chip >= 1)
    skipped = even & (chip >= 2)

    barrier = pltpu.get_barrier_semaphore()

    def greet(cond, other):
        @pl.when(cond)
        def _():
            pl.semaphore_signal(barrier, inc=1, device_id={"seq": other}, device_id_type=MESH)

    turns = range(1, chips - 1, 2)
    for c in turns:
        greet(me == 0, 2 * c)
    for cond, other in (
        (has_left, me - 1),
        (follows, me - 2),
        (relays, me + 2),
        (skipped, me - 3),
        (rejoined, 0),
        (held & odd, me + 4),
        (held & even, me + 5),
    ):
        greet(cond, other)
    loads = [
        pltpu.make_async_copy(src, dst, load_sem.at[i])
        for i, (src, dst) in enumerate(
            ((w_hbm, w_ref), (k_hbm, k_ref), (q_hbm, q_ref), (v_hbm, v_ref))
        )
    ]
    loads[3].start()
    loads[0].start()
    loads[1].start()
    smalls = [
        pltpu.make_async_copy(src, dst, small_sem.at[i])
        for i, (src, dst) in enumerate(
            ((beta_hbm, beta_ref), (seg_hbm, seg_ref), (visit_hbm, visit_ref))
        )
    ]
    for copy in smalls:
        copy.start()

    targets = (has_right, even & onward, bent, skips, detour, clears, clears)
    targets = targets + (me == 0,) * len(turns)

    @pl.when(has_right)
    def _():
        pl.semaphore_wait(barrier, sum(c.astype(jnp.int32) for c in targets))

    loads[3].wait()

    chunk = length // groups

    def remote(src, dst, send, recv, target):
        return pltpu.make_async_remote_copy(
            src_ref=src, dst_ref=dst, send_sem=send, recv_sem=recv,
            device_id={"seq": target}, device_id_type=MESH,
        )

    def rows_of(c):
        return pl.ds(c * chunk, chunk)

    def straight_copy(c, slot, target):
        return remote(
            v_ref.at[rows_of(c)], val_in.at[slot, rows_of(c)],
            own_send.at[c], val_recv.at[slot, c], target,
        )

    def bent_copy(c):
        return remote(
            v_hbm.at[rows_of(c)], relay_buf.at[rows_of(c)],
            own_send.at[c], relay_recv.at[c], me - 2,
        )

    def relay_copy(c):
        return remote(
            relay_buf.at[rows_of(c)], val_in.at[0, rows_of(c)],
            relay_send.at[c], val_recv.at[0, c], me + 3,
        )

    def pair_copy(src, slot):
        return remote(src, val_in.at[slot], pair_send.at[slot], pair_recv.at[slot], me + 1)

    pairs = [pair_copy(v_ref, 0), pair_copy(val_in.at[0], 1), pair_copy(val_in.at[1], 2)]
    skip = remote(v_hbm, val_in.at[2], skip_sems.at[0], skip_sems.at[1], me + 3)

    final = groups - 1

    def detour_copy(i):
        return remote(
            v_ref.at[rows_of(final)], hub_buf.at[i],
            own_send.at[final], hub_recv.at[i], 0,
        )

    def rejoin_copy(i, c):
        return remote(
            hub_buf.at[i], val_in.at[1, rows_of(final)],
            hub_send.at[i], val_recv.at[1, final], 2 * c + 2,
        )

    def relay_on(c):
        @pl.when(relays)
        def _():
            bent_copy(c).wait_recv()
            relay_copy(c).start()

    def far_copy(slot, p):
        part = pl.ds(p * sub, sub)
        return pltpu.make_async_remote_copy(
            src_ref=far_out.at[slot, part], dst_ref=far_in.at[slot, part],
            send_sem=far_send.at[slot, p], recv_sem=far_recv.at[slot, p],
            device_id={"seq": me + 1}, device_id_type=MESH,
        )

    ratio = group // sub

    def far_start(slot, g):
        @pl.when(has_right)
        def _():
            for i in range(ratio):
                far_copy(slot, g * ratio + i).start()

    def far_wait(slot, p):
        @pl.when(has_left)
        def _():
            far_copy(slot, p).wait_recv()

    @pl.when(odd & near_side & onward)
    def _():
        for c in range(groups):
            straight_copy(c, 0, me + 1).start()

    @pl.when(detour)
    def _():
        detour_copy(lax.div(chip, 2)).start()

    @pl.when(even & near_side & onward)
    def _():
        for c in range(groups):
            straight_copy(c, 1, me + 2).start()

    @pl.when(bent)
    def _():
        for c in range(groups):
            bent_copy(c).start()

    @pl.when(skips)
    def _():
        skip.start()

    @pl.when(even)
    def _():
        pairs[0].start()

    loads[2].start()

    @pl.when(me == 0)
    def _():
        far_in[...] = jnp.zeros_like(far_in)
        val_in[0] = jnp.zeros_like(val_in[0])
        val_in[1] = jnp.zeros_like(val_in[1])

    @pl.when(even & (chip < 2))
    def _():
        val_in[2] = jnp.zeros_like(val_in[2])

    rows = lax.broadcasted_iota(jnp.int32, (length, length), 0)
    lanes = lax.broadcasted_iota(jnp.int32, (length, length), 1)
    eye_f = (rows == lanes).astype(F32)
    eye_b = eye_f.astype(BF16)
    for copy in smalls:
        copy.wait()
    beta_rows[...] = beta_ref[...].astype(F32)

    seg_own = seg_ref[pl.ds(me, 1), :].astype(F32)
    seg_col = jnp.sum(jnp.where(rows == lanes, seg_own, 0.0), axis=1, keepdims=True)
    bias[0] = jnp.where((seg_own == seg_col) & (lanes <= rows), 0.0, -1e30)
    for r in range(1, depth + 1):
        seg_far = seg_ref[pl.ds(jnp.maximum(me - r, 0), 1), :].astype(F32)
        seen = jnp.where(visit_ref[0, r - 1] > 0, 0.0, -1e30) + jnp.where(me >= r, 0.0, -1e30)
        bias[r] = jnp.where(seg_far == seg_col, 0.0, -1e30) + seen

    def cols(h):
        return pl.ds(pl.multiple_of(h * width, width), width)

    def heads_of(g):
        return [g * group + i for i in range(group)]

    def prepare(g, carry):
        hs = heads_of(g)
        diag = rows == lanes
        ws = [w_ref[:, cols(h)] for h in hs]
        ks = [k_ref[:, cols(h)] for h in hs]
        grams = [nt(w, w) for w in ws]
        crosses = [nt(k, w) for k, w in zip(ks, ws)]
        rns = [
            1.0 / jnp.sqrt(jnp.sum(jnp.where(diag, m, 0.0), axis=0, keepdims=True) + EPSILON)
            for m in grams
        ]
        arows = [beta_rows[pl.ds(h, 1), :] * rn for h, rn in zip(hs, rns)]
        acols = [jnp.sum(jnp.where(diag, a, 0.0), axis=1, keepdims=True) for a in arows]
        lows = [
            jnp.where(rows > lanes, m * a * rn, 0.0) for m, a, rn in zip(grams, acols, rns)
        ]
        apart = rows ^ lanes
        xs = [eye_f - jnp.where(apart == 1, n, 0.0) for n in lows]
        step = 2
        while step < length:
            here = (apart >= step) & (apart < 2 * step)
            halves = [x.astype(BF16) for x in xs]
            lefts = [
                nn(x, jnp.where(here, n, 0.0).astype(BF16)) for x, n in zip(halves, lows)
            ]
            xs = [x - nn(y.astype(BF16), xb) for x, y, xb in zip(xs, lefts, halves)]
            step = step * 2
        halves = [x.astype(BF16) for x in xs]
        pairs = [split(n) for n in lows]
        rests = [
            (eye_f - xb.astype(F32)) - nn(wide(hi, lo), tall(xb, xb))
            for xb, (hi, lo) in zip(halves, pairs)
        ]
        fulls = [xb.astype(F32) + nn(xb, r.astype(BF16)) for xb, r in zip(halves, rests)]
        ms = [split(x * a) for x, a in zip(fulls, arows)]
        bs = [nn(wide(hi, lo), tall(w, w)) for (hi, lo), w in zip(ms, ws)]
        k2 = [split(jnp.where(lanes > rows, c, 0.0)) for c in crosses]
        cs = [
            nt(wide(chi, clo), wide(hi, hi)) + nt(chi, lo)
            for (chi, clo), (hi, lo) in zip(k2, ms)
        ]
        ds = [split(c * rn) for c, rn in zip(cs, rns)]
        moved = [
            k.astype(F32) - nn(wide(hi, lo), tall(w, w))
            for k, (hi, lo), w in zip(ks, ds, ws)
        ]
        for h, b, c, rn, m in zip(hs, bs, cs, rns, moved):
            far_out[0, h] = m.astype(BF16)
            back[h] = wide(*split(b))
            coef[h] = c
            rnorm[pl.ds(h, 1), :] = rn

        @pl.when(even | jnp.logical_not(held) | (g > late))
        def _():
            far_start(0, g)

        @pl.when(clears & (g == late))
        def _():
            for c in range(final):
                bent_copy(c).wait_send()
            for other in (me - 4, me - 5):
                pl.semaphore_signal(
                    clear_sem, inc=1, device_id={"seq": other}, device_id_type=MESH
                )

        @pl.when(held & (g == late))
        def _():
            pl.semaphore_wait(clear_sem, 1)

        @pl.when(odd & held & (g == late))
        def _():
            for i in range(late + 1):
                far_start(0, i)

        @pl.when(detour & (g == late))
        def _():
            for c in range(final):
                straight_copy(c, 1, me + 2).start()

        @pl.when(g >= groups // 2)
        def _():
            relay_on(g - groups // 2)

        @pl.when((me == 0) & (g == groups // 2))
        def _():
            for i, c in reversed(list(enumerate(turns))):
                detour_copy(i).wait_recv()
                rejoin_copy(i, c).start()

        return carry

    def advance(slot, g):
        hs = heads_of(g)
        for i in range(ratio):
            far_wait(slot, g * ratio + i)
        fs = [far_in[slot, h] for h in hs]
        inner = [nt(wide(f, f), back[h]) * rnorm[pl.ds(h, 1), :] for f, h in zip(fs, hs)]
        new = [
            f.astype(F32) - nn(y.astype(BF16), w_ref[:, cols(h)])
            for f, y, h in zip(fs, inner, hs)
        ]
        for h, x in zip(hs, new):
            far_out[slot + 1, h] = x.astype(BF16)
        far_start(slot + 1, g)

    def query(g):
        hs = heads_of(g)
        qs = [q_ref[:, cols(h)] for h in hs]
        gs = [
            split(jnp.where(lanes <= rows, nt(q, w_ref[:, cols(h)]) * rnorm[pl.ds(h, 1), :], 0.0))
            for q, h in zip(qs, hs)
        ]
        base = [nt(q, k_ref[:, cols(h)]) for q, h in zip(qs, hs)]
        for h, q, (hi, lo), s in zip(hs, qs, gs, base):
            b = back[h]
            bhi, blo = b[:, :width], b[:, width:]
            t = q.astype(F32) - (nn(wide(hi, lo), tall(bhi, bhi)) + nn(hi, blo))
            turned[h] = wide(*split(t * scale))
            chi, clo = split(coef[h])
            o = s - (nt(wide(hi, lo), wide(chi, chi)) + nt(hi, clo))
            own[h] = o * scale + bias[0]

    loads[0].wait()
    loads[1].wait()
    lax.fori_loop(0, groups, prepare, 0)


    def start(g):
        near = depth - 1
        for h in heads_of(g):
            t = turned[h]
            parts = [own[h]]
            for r in range(near):
                f = far_in[r, h]
                parts.append(nt(t, wide(f, f)) + bias[r + 1])
            top = jnp.max(functools.reduce(jnp.maximum, parts), axis=1, keepdims=True)
            ws = [jnp.exp(p - top) for p in parts]
            total = jnp.sum(functools.reduce(jnp.add, ws), axis=1, keepdims=True)
            tops[h] = jnp.broadcast_to(top, (length, width))
            sums[h] = jnp.broadcast_to(total, (length, width))
            vals = [v_ref[:, cols(h)]] + [val_in[r, :, cols(h)] for r in range(near)]
            own[h] = nn(wide(*[x.astype(BF16) for x in ws]), tall(*vals))

    def share_values():
        @pl.when(even & has_left)
        def _():
            for slot in range(2):
                for c in range(groups):
                    straight_copy(c, slot, me).wait_recv()

        @pl.when(even)
        def _():
            pairs[1].start()
            pairs[2].start()

    def first_hop(g, carry):
        query(g)
        advance(0, g)

        @pl.when((g >= 1) & (g <= groups // 2))
        def _():
            relay_on(g - 1 + groups - groups // 2)

        return carry

    def second_hop(g, carry):
        advance(1, g)

        @pl.when(odd & (g == 1))
        def _():
            pairs[0].wait_recv()
            pairs[1].wait_recv()

        @pl.when(g >= 1)
        def _():
            start(g - 1)

        return carry

    loads[2].wait()
    lax.fori_loop(0, groups, first_hop, 0)
    share_values()
    lax.fori_loop(0, groups, second_hop, 0)
    start(groups - 1)

    @pl.when(skipped)
    def _():
        skip.wait_recv()

    @pl.when(odd)
    def _():
        pairs[2].wait_recv()

    def finish(hs):
        last = depth - 1
        fs = [far_in[last, h] for h in hs]
        ss = [nt(turned[h], wide(f, f)) + bias[depth] for h, f in zip(hs, fs)]
        olds = [tops[h] for h in hs]
        news = [
            jnp.maximum(old, jnp.max(s, axis=1, keepdims=True)) for old, s in zip(olds, ss)
        ]
        ws = [jnp.exp(s - top) for s, top in zip(ss, news)]
        keeps = [jnp.exp(old - top) for old, top in zip(olds, news)]
        adds = [nn(w.astype(BF16), val_in[last, :, cols(h)]) for w, h in zip(ws, hs)]
        for h, w, keep, add in zip(hs, ws, keeps, adds):
            total = sums[h] * keep + jnp.sum(w, axis=1, keepdims=True)
            out_ref[:, cols(h)] = ((own[h] * keep + add) / total).astype(BF16)

    def finish_group(g, carry):
        for i in range(ratio):
            far_wait(depth - 1, g * ratio + i)
        finish(heads_of(g))
        return carry

    def finish_part(p, carry):
        far_wait(depth - 1, p)
        finish([p * sub + i for i in range(sub)])
        return carry

    lax.fori_loop(0, groups - 1, finish_group, 0)
    lax.fori_loop((groups - 1) * ratio, groups * ratio, finish_part, 0)

    @pl.when(has_right)
    def _():
        for slot in range(depth):
            for p in range(heads // sub):
                far_copy(slot, p).wait_send()

    @pl.when(onward & jnp.logical_not(clears))
    def _():
        for c in range(final):
            bent_copy(c).wait_send()

    @pl.when(onward)
    def _():
        bent_copy(final).wait_send()

    @pl.when(relays)
    def _():
        for c in range(groups):
            relay_copy(c).wait_send()

    @pl.when(me == 0)
    def _():
        for i, c in enumerate(turns):
            rejoin_copy(i, c).wait_send()

    @pl.when(skips)
    def _():
        skip.wait_send()

    @pl.when(even)
    def _():
        for copy in pairs:
            copy.wait_send()


def solution(mesh):
    blocks = mesh.shape["seq"]

    def shards(queries, keys, values, transitions, betas, segments, visits):
        length, total = queries.shape
        heads = betas.shape[1]
        width = total // heads
        depth = visits.shape[1]
        group = 4 if heads % 4 == 0 else 1
        sub = 2 if group % 2 == 0 else 1
        parts = heads // sub
        groups = heads // group
        turns = max(1, len(range(1, blocks // 2 - 1, 2)))
        anywhere = pl.BlockSpec(memory_space=pl.ANY)
        whole = pl.BlockSpec(memory_space=pltpu.VMEM)
        return pl.pallas_call(
            functools.partial(kernel, blocks, heads, group, sub),
            out_shape=pltpu.VMEM((length, total), BF16),
            in_specs=[anywhere] * 7,
            out_specs=whole,
            scratch_shapes=[pltpu.VMEM((length, total), BF16)] * 4 + [
                pltpu.VMEM((heads, length), BF16),
                pltpu.VMEM((blocks, length), jnp.int32),
                pltpu.SMEM((1, depth), jnp.int32),
                pltpu.VMEM((depth, heads, length, width), BF16),
                pltpu.VMEM((depth, heads, length, width), BF16),
                pltpu.VMEM((depth, length, total), BF16),
                pltpu.VMEM((length, total), BF16),
                pltpu.VMEM((turns, length // groups, total), BF16),
                pltpu.VMEM((heads, length, 2 * width), BF16),
                pltpu.VMEM((heads, length, length), F32),
                pltpu.VMEM((heads, length), F32),
                pltpu.VMEM((heads, length), F32),
                pltpu.VMEM((heads, length, 2 * width), BF16),
                pltpu.VMEM((heads, length, length), F32),
                pltpu.VMEM((heads, length, width), F32),
                pltpu.VMEM((heads, length, width), F32),
                pltpu.VMEM((depth + 1, length, length), F32),
                pltpu.SemaphoreType.DMA((depth, parts)),
                pltpu.SemaphoreType.DMA((depth, parts)),
                pltpu.SemaphoreType.DMA((groups,)),
                pltpu.SemaphoreType.DMA((depth, groups)),
                pltpu.SemaphoreType.DMA((groups,)),
                pltpu.SemaphoreType.DMA((groups,)),
                pltpu.SemaphoreType.DMA((turns,)),
                pltpu.SemaphoreType.DMA((turns,)),
                pltpu.SemaphoreType.DMA((depth,)),
                pltpu.SemaphoreType.DMA((depth,)),
                pltpu.SemaphoreType.DMA((2,)),
                pltpu.SemaphoreType.DMA((4,)),
                pltpu.SemaphoreType.DMA((3,)),
                pltpu.SemaphoreType.REGULAR,
            ],
            compiler_params=pltpu.CompilerParams(collective_id=0, has_side_effects=True),
        )(
            queries, keys, values, transitions, betas.T,
            segments.reshape(-1, length), visits,
        )

    return jax.shard_map(
        shards,
        mesh=mesh,
        in_specs=(
            P("seq", "head"),
            P("seq", "head"),
            P("seq", "head"),
            P("seq", "head"),
            P("seq", "head"),
            P(),
            P("seq", None),
        ),
        out_specs=P("seq", "head"),
        check_vma=False,
    )
```

```python
import functools

import jax
import jax.numpy as jnp
from jax import lax
from jax.experimental import pallas as pl
from jax.experimental.pallas import tpu as pltpu
from jax.sharding import PartitionSpec as P

EPSILON = 1e-06
MESH = pl.DeviceIdType.MESH
F32 = jnp.float32
BF16 = jnp.bfloat16


def nn(a, b):
    return lax.dot_general(a, b, (((1,), (0,)), ((), ())), preferred_element_type=F32)


def nt(a, b):
    return lax.dot_general(a, b, (((1,), (1,)), ((), ())), preferred_element_type=F32)


def split(x):
    hi = x.astype(BF16)
    return hi, (x - hi.astype(F32)).astype(BF16)


def wide(*parts):
    return jnp.concatenate(parts, axis=1)


def tall(*parts):
    return jnp.concatenate(parts, axis=0)


def kernel(
    blocks, heads, group, sub, q_hbm, k_hbm, v_hbm, w_hbm, beta_hbm, seg_hbm, visit_hbm, out_ref,
    q_ref, k_ref, v_ref, w_ref, beta_ref, seg_ref, visit_ref,
    far_in, far_out, val_in, relay_buf, hub_buf, back, coef, rnorm, beta_rows, turned, own, tops, sums, bias,
    far_send, far_recv, own_send, val_recv, relay_send, relay_recv, hub_send, hub_recv,
    pair_send, pair_recv, skip_sems, load_sem, small_sem, clear_sem,
):
    length = q_ref.shape[0]
    width = q_ref.shape[1] // heads
    depth = far_in.shape[0]
    groups = heads // group
    scale = width ** (-0.5)
    me = lax.axis_index("seq")
    odd = lax.rem(me, 2) == 1
    even = lax.rem(me, 2) == 0
    chip = lax.div(me, 2)
    chips = blocks // 2
    near_side = lax.rem(chip, 2) == 0
    far_side = lax.rem(chip, 2) == 1
    has_left = me >= 1
    has_right = me + 1 < blocks
    onward = chip + 1 < chips
    bent = odd & far_side & onward
    skips = odd & (chip + 2 < chips)
    relays = skips & near_side
    detour = even & far_side & onward
    clears = bent & (chip >= 3)
    held = far_side & (chip + 3 < chips)
    late = min(1, groups - 1)
    rejoined = even & near_side & (chip >= 2)
    follows = even & (chip >= 1)
    skipped = even & (chip >= 2)

    barrier = pltpu.get_barrier_semaphore()

    def greet(cond, other):
        @pl.when(cond)
        def _():
            pl.semaphore_signal(barrier, inc=1, device_id={"seq": other}, device_id_type=MESH)

    turns = range(1, chips - 1, 2)
    for c in turns:
        greet(me == 0, 2 * c)
    for cond, other in (
        (has_left, me - 1),
        (follows, me - 2),
        (relays, me + 2),
        (skipped, me - 3),
        (rejoined, 0),
        (held & odd, me + 4),
        (held & even, me + 5),
    ):
        greet(cond, other)
    loads = [
        pltpu.make_async_copy(src, dst, load_sem.at[i])
        for i, (src, dst) in enumerate(
            ((w_hbm, w_ref), (k_hbm, k_ref), (q_hbm, q_ref), (v_hbm, v_ref))
        )
    ]
    loads[3].start()
    loads[0].start()
    loads[1].start()
    smalls = [
        pltpu.make_async_copy(src, dst, small_sem.at[i])
        for i, (src, dst) in enumerate(
            ((beta_hbm, beta_ref), (seg_hbm, seg_ref), (visit_hbm, visit_ref))
        )
    ]
    for copy in smalls:
        copy.start()

    targets = (has_right, even & onward, bent, skips, detour, clears, clears)
    targets = targets + (me == 0,) * len(turns)

    @pl.when(has_right)
    def _():
        pl.semaphore_wait(barrier, sum(c.astype(jnp.int32) for c in targets))

    loads[3].wait()

    chunk = length // groups

    def remote(src, dst, send, recv, target):
        return pltpu.make_async_remote_copy(
            src_ref=src, dst_ref=dst, send_sem=send, recv_sem=recv,
            device_id={"seq": target}, device_id_type=MESH,
        )

    def rows_of(c):
        return pl.ds(c * chunk, chunk)

    def straight_copy(c, slot, target):
        return remote(
            v_ref.at[rows_of(c)], val_in.at[slot, rows_of(c)],
            own_send.at[c], val_recv.at[slot, c], target,
        )

    def bent_copy(c):
        return remote(
            v_hbm.at[rows_of(c)], relay_buf.at[rows_of(c)],
            own_send.at[c], relay_recv.at[c], me - 2,
        )

    def relay_copy(c):
        return remote(
            relay_buf.at[rows_of(c)], val_in.at[0, rows_of(c)],
            relay_send.at[c], val_recv.at[0, c], me + 3,
        )

    def pair_copy(src, slot):
        return remote(src, val_in.at[slot], pair_send.at[slot], pair_recv.at[slot], me + 1)

    pairs = [pair_copy(v_ref, 0), pair_copy(val_in.at[0], 1), pair_copy(val_in.at[1], 2)]
    skip = remote(v_hbm, val_in.at[2], skip_sems.at[0], skip_sems.at[1], me + 3)

    final = groups - 1

    def detour_copy(i):
        return remote(
            v_ref.at[rows_of(final)], hub_buf.at[i],
            own_send.at[final], hub_recv.at[i], 0,
        )

    def rejoin_copy(i, c):
        return remote(
            hub_buf.at[i], val_in.at[1, rows_of(final)],
            hub_send.at[i], val_recv.at[1, final], 2 * c + 2,
        )

    def relay_on(c):
        @pl.when(relays)
        def _():
            bent_copy(c).wait_recv()
            relay_copy(c).start()

    def far_copy(slot, p):
        part = pl.ds(p * sub, sub)
        return pltpu.make_async_remote_copy(
            src_ref=far_out.at[slot, part], dst_ref=far_in.at[slot, part],
            send_sem=far_send.at[slot, p], recv_sem=far_recv.at[slot, p],
            device_id={"seq": me + 1}, device_id_type=MESH,
        )

    ratio = group // sub

    def far_start(slot, g):
        @pl.when(has_right)
        def _():
            for i in range(ratio):
                far_copy(slot, g * ratio + i).start()

    def far_wait(slot, p):
        @pl.when(has_left)
        def _():
            far_copy(slot, p).wait_recv()

    @pl.when(odd & near_side & onward)
    def _():
        for c in range(groups):
            straight_copy(c, 0, me + 1).start()

    @pl.when(detour)
    def _():
        detour_copy(lax.div(chip, 2)).start()
        for c in range(min(1, final)):
            straight_copy(c, 1, me + 2).start()

    @pl.when(even & near_side & onward)
    def _():
        for c in range(groups):
            straight_copy(c, 1, me + 2).start()

    @pl.when(bent)
    def _():
        for c in range(groups):
            bent_copy(c).start()

    @pl.when(skips)
    def _():
        skip.start()

    @pl.when(even)
    def _():
        pairs[0].start()

    loads[2].start()

    @pl.when(me == 0)
    def _():
        far_in[...] = jnp.zeros_like(far_in)
        val_in[0] = jnp.zeros_like(val_in[0])
        val_in[1] = jnp.zeros_like(val_in[1])

    @pl.when(even & (chip < 2))
    def _():
        val_in[2] = jnp.zeros_like(val_in[2])

    rows = lax.broadcasted_iota(jnp.int32, (length, length), 0)
    lanes = lax.broadcasted_iota(jnp.int32, (length, length), 1)
    eye_f = (rows == lanes).astype(F32)
    eye_b = eye_f.astype(BF16)
    for copy in smalls:
        copy.wait()
    beta_rows[...] = beta_ref[...].astype(F32)

    seg_own = seg_ref[pl.ds(me, 1), :].astype(F32)
    seg_col = jnp.sum(jnp.where(rows == lanes, seg_own, 0.0), axis=1, keepdims=True)
    bias[0] = jnp.where((seg_own == seg_col) & (lanes <= rows), 0.0, -1e30)
    for r in range(1, depth + 1):
        seg_far = seg_ref[pl.ds(jnp.maximum(me - r, 0), 1), :].astype(F32)
        seen = jnp.where(visit_ref[0, r - 1] > 0, 0.0, -1e30) + jnp.where(me >= r, 0.0, -1e30)
        bias[r] = jnp.where(seg_far == seg_col, 0.0, -1e30) + seen

    def cols(h):
        return pl.ds(pl.multiple_of(h * width, width), width)

    def heads_of(g):
        return [g * group + i for i in range(group)]

    def prepare(g, carry):
        hs = heads_of(g)
        diag = rows == lanes
        ws = [w_ref[:, cols(h)] for h in hs]
        ks = [k_ref[:, cols(h)] for h in hs]
        grams = [nt(w, w) for w in ws]
        crosses = [nt(k, w) for k, w in zip(ks, ws)]
        rns = [
            1.0 / jnp.sqrt(jnp.sum(jnp.where(diag, m, 0.0), axis=0, keepdims=True) + EPSILON)
            for m in grams
        ]
        arows = [beta_rows[pl.ds(h, 1), :] * rn for h, rn in zip(hs, rns)]
        acols = [jnp.sum(jnp.where(diag, a, 0.0), axis=1, keepdims=True) for a in arows]
        lows = [
            jnp.where(rows > lanes, m * a * rn, 0.0) for m, a, rn in zip(grams, acols, rns)
        ]
        apart = rows ^ lanes
        xs = [eye_f - jnp.where(apart == 1, n, 0.0) for n in lows]
        step = 2
        while step < length:
            here = (apart >= step) & (apart < 2 * step)
            halves = [x.astype(BF16) for x in xs]
            lefts = [
                nn(x, jnp.where(here, n, 0.0).astype(BF16)) for x, n in zip(halves, lows)
            ]
            xs = [x - nn(y.astype(BF16), xb) for x, y, xb in zip(xs, lefts, halves)]
            step = step * 2
        halves = [x.astype(BF16) for x in xs]
        pairs = [split(n) for n in lows]
        rests = [
            (eye_f - xb.astype(F32)) - nn(wide(hi, lo), tall(xb, xb))
            for xb, (hi, lo) in zip(halves, pairs)
        ]
        fulls = [xb.astype(F32) + nn(xb, r.astype(BF16)) for xb, r in zip(halves, rests)]
        ms = [split(x * a) for x, a in zip(fulls, arows)]
        bs = [nn(wide(hi, lo), tall(w, w)) for (hi, lo), w in zip(ms, ws)]
        k2 = [split(jnp.where(lanes > rows, c, 0.0)) for c in crosses]
        cs = [
            nt(wide(chi, clo), wide(hi, hi)) + nt(chi, lo)
            for (chi, clo), (hi, lo) in zip(k2, ms)
        ]
        ds = [split(c * rn) for c, rn in zip(cs, rns)]
        moved = [
            k.astype(F32) - nn(wide(hi, lo), tall(w, w))
            for k, (hi, lo), w in zip(ks, ds, ws)
        ]
        for h, b, c, rn, m in zip(hs, bs, cs, rns, moved):
            far_out[0, h] = m.astype(BF16)
            back[h] = wide(*split(b))
            coef[h] = c
            rnorm[pl.ds(h, 1), :] = rn

        @pl.when(even | jnp.logical_not(held) | (g > late))
        def _():
            far_start(0, g)

        @pl.when(clears & (g == late))
        def _():
            for c in range(final):
                bent_copy(c).wait_send()
            for other in (me - 4, me - 5):
                pl.semaphore_signal(
                    clear_sem, inc=1, device_id={"seq": other}, device_id_type=MESH
                )

        @pl.when(held & (g == late))
        def _():
            pl.semaphore_wait(clear_sem, 1)

        @pl.when(odd & held & (g == late))
        def _():
            for i in range(late + 1):
                far_start(0, i)

        @pl.when(detour & (g == late))
        def _():
            for c in range(1, final):
                straight_copy(c, 1, me + 2).start()

        @pl.when(g >= late)
        def _():
            relay_on(g - late)

        @pl.when((me == 0) & (g == groups // 2))
        def _():
            for i, c in reversed(list(enumerate(turns))):
                detour_copy(i).wait_recv()
                rejoin_copy(i, c).start()

        return carry

    def advance(slot, g):
        hs = heads_of(g)
        for i in range(ratio):
            far_wait(slot, g * ratio + i)
        fs = [far_in[slot, h] for h in hs]
        inner = [nt(wide(f, f), back[h]) * rnorm[pl.ds(h, 1), :] for f, h in zip(fs, hs)]
        new = [
            f.astype(F32) - nn(y.astype(BF16), w_ref[:, cols(h)])
            for f, y, h in zip(fs, inner, hs)
        ]
        for h, x in zip(hs, new):
            far_out[slot + 1, h] = x.astype(BF16)
        far_start(slot + 1, g)

    def query(g):
        hs = heads_of(g)
        qs = [q_ref[:, cols(h)] for h in hs]
        gs = [
            split(jnp.where(lanes <= rows, nt(q, w_ref[:, cols(h)]) * rnorm[pl.ds(h, 1), :], 0.0))
            for q, h in zip(qs, hs)
        ]
        base = [nt(q, k_ref[:, cols(h)]) for q, h in zip(qs, hs)]
        for h, q, (hi, lo), s in zip(hs, qs, gs, base):
            b = back[h]
            bhi, blo = b[:, :width], b[:, width:]
            t = q.astype(F32) - (nn(wide(hi, lo), tall(bhi, bhi)) + nn(hi, blo))
            turned[h] = wide(*split(t * scale))
            chi, clo = split(coef[h])
            o = s - (nt(wide(hi, lo), wide(chi, chi)) + nt(hi, clo))
            own[h] = o * scale + bias[0]

    loads[0].wait()
    loads[1].wait()
    lax.fori_loop(0, groups, prepare, 0)


    def start(g):
        near = depth - 1
        for h in heads_of(g):
            t = turned[h]
            parts = [own[h]]
            for r in range(near):
                f = far_in[r, h]
                parts.append(nt(t, wide(f, f)) + bias[r + 1])
            top = jnp.max(functools.reduce(jnp.maximum, parts), axis=1, keepdims=True)
            ws = [jnp.exp(p - top) for p in parts]
            total = jnp.sum(functools.reduce(jnp.add, ws), axis=1, keepdims=True)
            tops[h] = jnp.broadcast_to(top, (length, width))
            sums[h] = jnp.broadcast_to(total, (length, width))
            vals = [v_ref[:, cols(h)]] + [val_in[r, :, cols(h)] for r in range(near)]
            own[h] = nn(wide(*[x.astype(BF16) for x in ws]), tall(*vals))

    def share_values(slot):
        @pl.when(even & has_left)
        def _():
            for c in range(groups):
                straight_copy(c, slot, me).wait_recv()

        @pl.when(even)
        def _():
            pairs[slot + 1].start()

    def first_hop(g, carry):
        query(g)
        advance(0, g)

        @pl.when(g < late)
        def _():
            relay_on(g + groups - late)

        return carry

    def second_hop(g, carry):
        advance(1, g)

        @pl.when(g == late)
        def _():
            share_values(1)

        @pl.when(odd & (g == late))
        def _():
            pairs[0].wait_recv()
            pairs[1].wait_recv()

        @pl.when(g >= 1)
        def _():
            start(g - 1)

        return carry

    loads[2].wait()
    lax.fori_loop(0, groups, first_hop, 0)
    share_values(0)
    lax.fori_loop(0, groups, second_hop, 0)
    start(groups - 1)

    @pl.when(skipped)
    def _():
        skip.wait_recv()

    @pl.when(odd)
    def _():
        pairs[2].wait_recv()

    def finish(hs):
        last = depth - 1
        fs = [far_in[last, h] for h in hs]
        ss = [nt(turned[h], wide(f, f)) + bias[depth] for h, f in zip(hs, fs)]
        olds = [tops[h] for h in hs]
        news = [
            jnp.maximum(old, jnp.max(s, axis=1, keepdims=True)) for old, s in zip(olds, ss)
        ]
        ws = [jnp.exp(s - top) for s, top in zip(ss, news)]
        keeps = [jnp.exp(old - top) for old, top in zip(olds, news)]
        adds = [nn(w.astype(BF16), val_in[last, :, cols(h)]) for w, h in zip(ws, hs)]
        for h, w, keep, add in zip(hs, ws, keeps, adds):
            total = sums[h] * keep + jnp.sum(w, axis=1, keepdims=True)
            out_ref[:, cols(h)] = ((own[h] * keep + add) / total).astype(BF16)

    def finish_group(g, carry):
        for i in range(ratio):
            far_wait(depth - 1, g * ratio + i)
        finish(heads_of(g))
        return carry

    def finish_part(p, carry):
        far_wait(depth - 1, p)
        finish([p * sub + i for i in range(sub)])
        return carry

    lax.fori_loop(0, groups - 1, finish_group, 0)
    lax.fori_loop((groups - 1) * ratio, groups * ratio, finish_part, 0)

    @pl.when(has_right)
    def _():
        for slot in range(depth):
            for p in range(heads // sub):
                far_copy(slot, p).wait_send()

    @pl.when(onward & jnp.logical_not(clears))
    def _():
        for c in range(final):
            bent_copy(c).wait_send()

    @pl.when(onward)
    def _():
        bent_copy(final).wait_send()

    @pl.when(relays)
    def _():
        for c in range(groups):
            relay_copy(c).wait_send()

    @pl.when(me == 0)
    def _():
        for i, c in enumerate(turns):
            rejoin_copy(i, c).wait_send()

    @pl.when(skips)
    def _():
        skip.wait_send()

    @pl.when(even)
    def _():
        for copy in pairs:
            copy.wait_send()


def solution(mesh):
    blocks = mesh.shape["seq"]

    def shards(queries, keys, values, transitions, betas, segments, visits):
        length, total = queries.shape
        heads = betas.shape[1]
        width = total // heads
        depth = visits.shape[1]
        group = 4 if heads % 4 == 0 else 1
        sub = 2 if group % 2 == 0 else 1
        parts = heads // sub
        groups = heads // group
        turns = max(1, len(range(1, blocks // 2 - 1, 2)))
        anywhere = pl.BlockSpec(memory_space=pl.ANY)
        whole = pl.BlockSpec(memory_space=pltpu.VMEM)
        return pl.pallas_call(
            functools.partial(kernel, blocks, heads, group, sub),
            out_shape=pltpu.VMEM((length, total), BF16),
            in_specs=[anywhere] * 7,
            out_specs=whole,
            scratch_shapes=[pltpu.VMEM((length, total), BF16)] * 4 + [
                pltpu.VMEM((heads, length), BF16),
                pltpu.VMEM((blocks, length), jnp.int32),
                pltpu.SMEM((1, depth), jnp.int32),
                pltpu.VMEM((depth, heads, length, width), BF16),
                pltpu.VMEM((depth, heads, length, width), BF16),
                pltpu.VMEM((depth, length, total), BF16),
                pltpu.VMEM((length, total), BF16),
                pltpu.VMEM((turns, length // groups, total), BF16),
                pltpu.VMEM((heads, length, 2 * width), BF16),
                pltpu.VMEM((heads, length, length), F32),
                pltpu.VMEM((heads, length), F32),
                pltpu.VMEM((heads, length), F32),
                pltpu.VMEM((heads, length, 2 * width), BF16),
                pltpu.VMEM((heads, length, length), F32),
                pltpu.VMEM((heads, length, width), F32),
                pltpu.VMEM((heads, length, width), F32),
                pltpu.VMEM((depth + 1, length, length), F32),
                pltpu.SemaphoreType.DMA((depth, parts)),
                pltpu.SemaphoreType.DMA((depth, parts)),
                pltpu.SemaphoreType.DMA((groups,)),
                pltpu.SemaphoreType.DMA((depth, groups)),
                pltpu.SemaphoreType.DMA((groups,)),
                pltpu.SemaphoreType.DMA((groups,)),
                pltpu.SemaphoreType.DMA((turns,)),
                pltpu.SemaphoreType.DMA((turns,)),
                pltpu.SemaphoreType.DMA((depth,)),
                pltpu.SemaphoreType.DMA((depth,)),
                pltpu.SemaphoreType.DMA((2,)),
                pltpu.SemaphoreType.DMA((4,)),
                pltpu.SemaphoreType.DMA((3,)),
                pltpu.SemaphoreType.REGULAR,
            ],
            compiler_params=pltpu.CompilerParams(collective_id=0, has_side_effects=True),
        )(
            queries, keys, values, transitions, betas.T,
            segments.reshape(-1, length), visits,
        )

    return jax.shard_map(
        shards,
        mesh=mesh,
        in_specs=(
            P("seq", "head"),
            P("seq", "head"),
            P("seq", "head"),
            P("seq", "head"),
            P("seq", "head"),
            P(),
            P("seq", None),
        ),
        out_specs=P("seq", "head"),
        check_vma=False,
    )
```

```python
import functools

import jax
import jax.numpy as jnp
from jax import lax
from jax.experimental import pallas as pl
from jax.experimental.pallas import tpu as pltpu
from jax.sharding import PartitionSpec as P

EPSILON = 1e-06
MESH = pl.DeviceIdType.MESH
F32 = jnp.float32
BF16 = jnp.bfloat16


def nn(a, b):
    return lax.dot_general(a, b, (((1,), (0,)), ((), ())), preferred_element_type=F32)


def nt(a, b):
    return lax.dot_general(a, b, (((1,), (1,)), ((), ())), preferred_element_type=F32)


def split(x):
    hi = x.astype(BF16)
    return hi, (x - hi.astype(F32)).astype(BF16)


def wide(*parts):
    return jnp.concatenate(parts, axis=1)


def tall(*parts):
    return jnp.concatenate(parts, axis=0)


def kernel(
    blocks, heads, group, sub, q_hbm, k_hbm, v_hbm, w_hbm, beta_hbm, seg_hbm, visit_hbm, out_ref,
    q_ref, k_ref, v_ref, w_ref, beta_ref, seg_ref, visit_ref,
    far_in, far_out, val_in, relay_buf, hub_buf, back, coef, rnorm, beta_rows, turned, own, tops, sums, bias,
    far_send, far_recv, own_send, val_recv, relay_send, relay_recv, hub_send, hub_recv,
    pair_send, pair_recv, skip_sems, load_sem, small_sem, clear_sem,
):
    length = q_ref.shape[0]
    width = q_ref.shape[1] // heads
    depth = far_in.shape[0]
    groups = heads // group
    scale = width ** (-0.5)
    me = lax.axis_index("seq")
    odd = lax.rem(me, 2) == 1
    even = lax.rem(me, 2) == 0
    chip = lax.div(me, 2)
    chips = blocks // 2
    near_side = lax.rem(chip, 2) == 0
    far_side = lax.rem(chip, 2) == 1
    has_left = me >= 1
    has_right = me + 1 < blocks
    onward = chip + 1 < chips
    bent = odd & far_side & onward
    skips = odd & (chip + 2 < chips)
    relays = skips & near_side
    detour = even & far_side & onward
    clears = bent & (chip >= 3)
    held = far_side & (chip + 3 < chips)
    late = min(1, groups - 1)
    rejoined = even & near_side & (chip >= 2)
    follows = even & (chip >= 1)
    skipped = even & (chip >= 2)

    barrier = pltpu.get_barrier_semaphore()

    def greet(cond, other):
        @pl.when(cond)
        def _():
            pl.semaphore_signal(barrier, inc=1, device_id={"seq": other}, device_id_type=MESH)

    turns = range(1, chips - 1, 2)
    for c in turns:
        greet(me == 0, 2 * c)
    for cond, other in (
        (has_left, me - 1),
        (follows, me - 2),
        (relays, me + 2),
        (skipped, me - 3),
        (rejoined, 0),
        (held & odd, me + 4),
        (held & even, me + 5),
    ):
        greet(cond, other)
    loads = [
        pltpu.make_async_copy(src, dst, load_sem.at[i])
        for i, (src, dst) in enumerate(
            ((w_hbm, w_ref), (k_hbm, k_ref), (q_hbm, q_ref), (v_hbm, v_ref))
        )
    ]
    loads[3].start()
    loads[0].start()
    loads[1].start()
    smalls = [
        pltpu.make_async_copy(src, dst, small_sem.at[i])
        for i, (src, dst) in enumerate(
            ((beta_hbm, beta_ref), (seg_hbm, seg_ref), (visit_hbm, visit_ref))
        )
    ]
    for copy in smalls:
        copy.start()

    targets = (has_right, even & onward, bent, skips, detour, clears, clears)
    targets = targets + (me == 0,) * len(turns)

    @pl.when(has_right)
    def _():
        pl.semaphore_wait(barrier, sum(c.astype(jnp.int32) for c in targets))

    loads[3].wait()

    chunk = length // groups

    def remote(src, dst, send, recv, target):
        return pltpu.make_async_remote_copy(
            src_ref=src, dst_ref=dst, send_sem=send, recv_sem=recv,
            device_id={"seq": target}, device_id_type=MESH,
        )

    def rows_of(c):
        return pl.ds(c * chunk, chunk)

    def straight_copy(c, slot, target):
        return remote(
            v_ref.at[rows_of(c)], val_in.at[slot, rows_of(c)],
            own_send.at[c], val_recv.at[slot, c], target,
        )

    def bent_copy(c):
        return remote(
            v_hbm.at[rows_of(c)], relay_buf.at[rows_of(c)],
            own_send.at[c], relay_recv.at[c], me - 2,
        )

    def relay_copy(c):
        return remote(
            relay_buf.at[rows_of(c)], val_in.at[0, rows_of(c)],
            relay_send.at[c], val_recv.at[0, c], me + 3,
        )

    def pair_copy(src, slot):
        return remote(src, val_in.at[slot], pair_send.at[slot], pair_recv.at[slot], me + 1)

    pairs = [pair_copy(v_ref, 0), pair_copy(val_in.at[0], 1), pair_copy(val_in.at[1], 2)]
    skip = remote(v_hbm, val_in.at[2], skip_sems.at[0], skip_sems.at[1], me + 3)

    final = groups - 1

    def detour_copy(i):
        return remote(
            v_ref.at[rows_of(final)], hub_buf.at[i],
            own_send.at[final], hub_recv.at[i], 0,
        )

    def rejoin_copy(i, c):
        return remote(
            hub_buf.at[i], val_in.at[1, rows_of(final)],
            hub_send.at[i], val_recv.at[1, final], 2 * c + 2,
        )

    def relay_on(c):
        @pl.when(relays)
        def _():
            bent_copy(c).wait_recv()
            relay_copy(c).start()

    def far_copy(slot, p):
        part = pl.ds(p * sub, sub)
        return pltpu.make_async_remote_copy(
            src_ref=far_out.at[slot, part], dst_ref=far_in.at[slot, part],
            send_sem=far_send.at[slot, p], recv_sem=far_recv.at[slot, p],
            device_id={"seq": me + 1}, device_id_type=MESH,
        )

    ratio = group // sub

    def far_start(slot, g):
        @pl.when(has_right)
        def _():
            for i in range(ratio):
                far_copy(slot, g * ratio + i).start()

    def far_wait(slot, p):
        @pl.when(has_left)
        def _():
            far_copy(slot, p).wait_recv()

    @pl.when(odd & near_side & onward)
    def _():
        for c in range(groups):
            straight_copy(c, 0, me + 1).start()

    @pl.when(detour)
    def _():
        detour_copy(lax.div(chip, 2)).start()
        for c in range(min(1, final)):
            straight_copy(c, 1, me + 2).start()

    @pl.when(even & near_side & onward)
    def _():
        for c in range(groups):
            straight_copy(c, 1, me + 2).start()

    @pl.when(bent)
    def _():
        for c in range(groups):
            bent_copy(c).start()

    @pl.when(skips)
    def _():
        skip.start()

    @pl.when(even)
    def _():
        pairs[0].start()

    loads[2].start()

    @pl.when(me == 0)
    def _():
        far_in[...] = jnp.zeros_like(far_in)
        val_in[0] = jnp.zeros_like(val_in[0])
        val_in[1] = jnp.zeros_like(val_in[1])

    @pl.when(even & (chip < 2))
    def _():
        val_in[2] = jnp.zeros_like(val_in[2])

    rows = lax.broadcasted_iota(jnp.int32, (length, length), 0)
    lanes = lax.broadcasted_iota(jnp.int32, (length, length), 1)
    eye_f = (rows == lanes).astype(F32)
    eye_b = eye_f.astype(BF16)
    for copy in smalls:
        copy.wait()
    beta_rows[...] = beta_ref[...].astype(F32)

    seg_own = seg_ref[pl.ds(me, 1), :].astype(F32)
    seg_col = jnp.sum(jnp.where(rows == lanes, seg_own, 0.0), axis=1, keepdims=True)
    bias[0] = jnp.where((seg_own == seg_col) & (lanes <= rows), 0.0, -1e30)
    for r in range(1, depth + 1):
        seg_far = seg_ref[pl.ds(jnp.maximum(me - r, 0), 1), :].astype(F32)
        seen = jnp.where(visit_ref[0, r - 1] > 0, 0.0, -1e30) + jnp.where(me >= r, 0.0, -1e30)
        bias[r] = jnp.where(seg_far == seg_col, 0.0, -1e30) + seen

    def cols(h):
        return pl.ds(pl.multiple_of(h * width, width), width)

    def heads_of(g):
        return [g * group + i for i in range(group)]

    def prepare(g, carry):
        hs = heads_of(g)
        diag = rows == lanes
        ws = [w_ref[:, cols(h)] for h in hs]
        ks = [k_ref[:, cols(h)] for h in hs]
        grams = [nt(w, w) for w in ws]
        crosses = [nt(k, w) for k, w in zip(ks, ws)]
        rns = [
            1.0 / jnp.sqrt(jnp.sum(jnp.where(diag, m, 0.0), axis=0, keepdims=True) + EPSILON)
            for m in grams
        ]
        arows = [beta_rows[pl.ds(h, 1), :] * rn for h, rn in zip(hs, rns)]
        acols = [jnp.sum(jnp.where(diag, a, 0.0), axis=1, keepdims=True) for a in arows]
        lows = [
            jnp.where(rows > lanes, m * a * rn, 0.0) for m, a, rn in zip(grams, acols, rns)
        ]
        apart = rows ^ lanes
        xs = [eye_f - jnp.where(apart == 1, n, 0.0) for n in lows]
        step = 2
        while step < length:
            here = (apart >= step) & (apart < 2 * step)
            halves = [x.astype(BF16) for x in xs]
            lefts = [
                nn(x, jnp.where(here, n, 0.0).astype(BF16)) for x, n in zip(halves, lows)
            ]
            xs = [x - nn(y.astype(BF16), xb) for x, y, xb in zip(xs, lefts, halves)]
            step = step * 2
        halves = [x.astype(BF16) for x in xs]
        pairs = [split(n) for n in lows]
        rests = [
            (eye_f - xb.astype(F32)) - nn(wide(hi, lo), tall(xb, xb))
            for xb, (hi, lo) in zip(halves, pairs)
        ]
        fulls = [xb.astype(F32) + nn(xb, r.astype(BF16)) for xb, r in zip(halves, rests)]
        ms = [split(x * a) for x, a in zip(fulls, arows)]
        bs = [nn(wide(hi, lo), tall(w, w)) for (hi, lo), w in zip(ms, ws)]
        k2 = [split(jnp.where(lanes > rows, c, 0.0)) for c in crosses]
        cs = [
            nt(wide(chi, clo), wide(hi, hi)) + nt(chi, lo)
            for (chi, clo), (hi, lo) in zip(k2, ms)
        ]
        ds = [split(c * rn) for c, rn in zip(cs, rns)]
        moved = [
            k.astype(F32) - nn(wide(hi, lo), tall(w, w))
            for k, (hi, lo), w in zip(ks, ds, ws)
        ]
        for h, b, c, rn, m in zip(hs, bs, cs, rns, moved):
            far_out[0, h] = m.astype(BF16)
            back[h] = wide(*split(b))
            coef[h] = c
            rnorm[pl.ds(h, 1), :] = rn

        @pl.when(even | jnp.logical_not(held) | (g > late))
        def _():
            far_start(0, g)

        @pl.when(clears & (g == late))
        def _():
            for c in range(final):
                bent_copy(c).wait_send()
            for other in (me - 4, me - 5):
                pl.semaphore_signal(
                    clear_sem, inc=1, device_id={"seq": other}, device_id_type=MESH
                )

        @pl.when(held & (g == late))
        def _():
            pl.semaphore_wait(clear_sem, 1)

        @pl.when(odd & held & (g == late))
        def _():
            for i in range(late + 1):
                far_start(0, i)

        @pl.when(detour & (g == late))
        def _():
            for c in range(1, final):
                straight_copy(c, 1, me + 2).start()

        @pl.when(g >= late)
        def _():
            relay_on(g - late)

        @pl.when((me == 0) & (g == groups // 2))
        def _():
            for i, c in reversed(list(enumerate(turns))):
                detour_copy(i).wait_recv()
                rejoin_copy(i, c).start()

        return carry

    def advance(slot, g):
        hs = heads_of(g)
        for i in range(ratio):
            far_wait(slot, g * ratio + i)
        fs = [far_in[slot, h] for h in hs]
        inner = [nt(wide(f, f), back[h]) * rnorm[pl.ds(h, 1), :] for f, h in zip(fs, hs)]
        new = [
            f.astype(F32) - nn(y.astype(BF16), w_ref[:, cols(h)])
            for f, y, h in zip(fs, inner, hs)
        ]
        for h, x in zip(hs, new):
            far_out[slot + 1, h] = x.astype(BF16)
        far_start(slot + 1, g)

    def query(g):
        hs = heads_of(g)
        qs = [q_ref[:, cols(h)] for h in hs]
        gs = [
            split(jnp.where(lanes <= rows, nt(q, w_ref[:, cols(h)]) * rnorm[pl.ds(h, 1), :], 0.0))
            for q, h in zip(qs, hs)
        ]
        base = [nt(q, k_ref[:, cols(h)]) for q, h in zip(qs, hs)]
        for h, q, (hi, lo), s in zip(hs, qs, gs, base):
            b = back[h]
            bhi, blo = b[:, :width], b[:, width:]
            t = q.astype(F32) - (nn(wide(hi, lo), tall(bhi, bhi)) + nn(hi, blo))
            turned[h] = wide(*split(t * scale))
            chi, clo = split(coef[h])
            o = s - (nt(wide(hi, lo), wide(chi, chi)) + nt(hi, clo))
            own[h] = o * scale + bias[0]

    loads[0].wait()
    loads[1].wait()
    lax.fori_loop(0, groups, prepare, 0)


    def start(g):
        near = depth - 1
        for h in heads_of(g):
            t = turned[h]
            parts = [own[h]]
            for r in range(near):
                f = far_in[r, h]
                parts.append(nt(t, wide(f, f)) + bias[r + 1])
            top = jnp.max(functools.reduce(jnp.maximum, parts), axis=1, keepdims=True)
            ws = [jnp.exp(p - top) for p in parts]
            total = jnp.sum(functools.reduce(jnp.add, ws), axis=1, keepdims=True)
            tops[h] = jnp.broadcast_to(top, (length, width))
            sums[h] = jnp.broadcast_to(total, (length, width))
            vals = [v_ref[:, cols(h)]] + [val_in[r, :, cols(h)] for r in range(near)]
            own[h] = nn(wide(*[x.astype(BF16) for x in ws]), tall(*vals))

    def share_values(slot):
        @pl.when(even & has_left)
        def _():
            for c in range(groups):
                straight_copy(c, slot, me).wait_recv()

        @pl.when(even)
        def _():
            pairs[slot + 1].start()

    def first_hop(g, carry):
        query(g)
        advance(0, g)

        @pl.when(g < late)
        def _():
            relay_on(g + groups - late)

        return carry

    def second_hop(g, carry):
        advance(1, g)

        @pl.when(g == late)
        def _():
            share_values(1)

        @pl.when(odd & (g == late))
        def _():
            pairs[0].wait_recv()
            pairs[1].wait_recv()

        @pl.when(g >= 1)
        def _():
            start(g - 1)

        return carry

    loads[2].wait()
    lax.fori_loop(0, groups, first_hop, 0)
    share_values(0)
    lax.fori_loop(0, groups, second_hop, 0)
    start(groups - 1)

    @pl.when(skipped)
    def _():
        skip.wait_recv()

    @pl.when(odd)
    def _():
        pairs[2].wait_recv()

    def finish(hs):
        last = depth - 1
        fs = [far_in[last, h] for h in hs]
        ss = [nt(turned[h], wide(f, f)) + bias[depth] for h, f in zip(hs, fs)]
        olds = [tops[h] for h in hs]
        news = [
            jnp.maximum(old, jnp.max(s, axis=1, keepdims=True)) for old, s in zip(olds, ss)
        ]
        ws = [jnp.exp(s - top) for s, top in zip(ss, news)]
        keeps = [jnp.exp(old - top) for old, top in zip(olds, news)]
        adds = [nn(w.astype(BF16), val_in[last, :, cols(h)]) for w, h in zip(ws, hs)]
        for h, w, keep, add in zip(hs, ws, keeps, adds):
            total = sums[h] * keep + jnp.sum(w, axis=1, keepdims=True)
            out_ref[:, cols(h)] = ((own[h] * keep + add) / total).astype(BF16)

    def finish_group(g, carry):
        for i in range(ratio):
            far_wait(depth - 1, g * ratio + i)
        finish(heads_of(g))
        return carry

    def finish_part(p, carry):
        far_wait(depth - 1, p)
        finish([p * sub + i for i in range(sub)])
        return carry

    lax.fori_loop(0, groups - 1, finish_group, 0)
    lax.fori_loop((groups - 1) * ratio, groups * ratio, finish_part, 0)

    @pl.when(has_right)
    def _():
        for slot in range(depth):
            for p in range(heads // sub):
                far_copy(slot, p).wait_send()

    @pl.when(onward & jnp.logical_not(clears))
    def _():
        for c in range(final):
            bent_copy(c).wait_send()

    @pl.when(onward)
    def _():
        bent_copy(final).wait_send()

    @pl.when(relays)
    def _():
        for c in range(groups):
            relay_copy(c).wait_send()

    @pl.when(me == 0)
    def _():
        for i, c in enumerate(turns):
            rejoin_copy(i, c).wait_send()

    @pl.when(skips)
    def _():
        skip.wait_send()

    @pl.when(even)
    def _():
        for copy in pairs:
            copy.wait_send()


def solution(mesh):
    blocks = mesh.shape["seq"]

    def shards(queries, keys, values, transitions, betas, segments, visits):
        length, total = queries.shape
        heads = betas.shape[1]
        width = total // heads
        depth = visits.shape[1]
        group = 4 if heads % 4 == 0 else 1
        sub = group
        parts = heads // sub
        groups = heads // group
        turns = max(1, len(range(1, blocks // 2 - 1, 2)))
        anywhere = pl.BlockSpec(memory_space=pl.ANY)
        whole = pl.BlockSpec(memory_space=pltpu.VMEM)
        return pl.pallas_call(
            functools.partial(kernel, blocks, heads, group, sub),
            out_shape=pltpu.VMEM((length, total), BF16),
            in_specs=[anywhere] * 7,
            out_specs=whole,
            scratch_shapes=[pltpu.VMEM((length, total), BF16)] * 4 + [
                pltpu.VMEM((heads, length), BF16),
                pltpu.VMEM((blocks, length), jnp.int32),
                pltpu.SMEM((1, depth), jnp.int32),
                pltpu.VMEM((depth, heads, length, width), BF16),
                pltpu.VMEM((depth, heads, length, width), BF16),
                pltpu.VMEM((depth, length, total), BF16),
                pltpu.VMEM((length, total), BF16),
                pltpu.VMEM((turns, length // groups, total), BF16),
                pltpu.VMEM((heads, length, 2 * width), BF16),
                pltpu.VMEM((heads, length, length), F32),
                pltpu.VMEM((heads, length), F32),
                pltpu.VMEM((heads, length), F32),
                pltpu.VMEM((heads, length, 2 * width), BF16),
                pltpu.VMEM((heads, length, length), F32),
                pltpu.VMEM((heads, length, width), F32),
                pltpu.VMEM((heads, length, width), F32),
                pltpu.VMEM((depth + 1, length, length), F32),
                pltpu.SemaphoreType.DMA((depth, parts)),
                pltpu.SemaphoreType.DMA((depth, parts)),
                pltpu.SemaphoreType.DMA((groups,)),
                pltpu.SemaphoreType.DMA((depth, groups)),
                pltpu.SemaphoreType.DMA((groups,)),
                pltpu.SemaphoreType.DMA((groups,)),
                pltpu.SemaphoreType.DMA((turns,)),
                pltpu.SemaphoreType.DMA((turns,)),
                pltpu.SemaphoreType.DMA((depth,)),
                pltpu.SemaphoreType.DMA((depth,)),
                pltpu.SemaphoreType.DMA((2,)),
                pltpu.SemaphoreType.DMA((4,)),
                pltpu.SemaphoreType.DMA((3,)),
                pltpu.SemaphoreType.REGULAR,
            ],
            compiler_params=pltpu.CompilerParams(collective_id=0, has_side_effects=True),
        )(
            queries, keys, values, transitions, betas.T,
            segments.reshape(-1, length), visits,
        )

    return jax.shard_map(
        shards,
        mesh=mesh,
        in_specs=(
            P("seq", "head"),
            P("seq", "head"),
            P("seq", "head"),
            P("seq", "head"),
            P("seq", "head"),
            P(),
            P("seq", None),
        ),
        out_specs=P("seq", "head"),
        check_vma=False,
    )
```

```python
import functools

import jax
import jax.numpy as jnp
from jax import lax
from jax.experimental import pallas as pl
from jax.experimental.pallas import tpu as pltpu
from jax.sharding import PartitionSpec as P

EPSILON = 1e-06
MESH = pl.DeviceIdType.MESH
F32 = jnp.float32
BF16 = jnp.bfloat16


def nn(a, b):
    return lax.dot_general(a, b, (((1,), (0,)), ((), ())), preferred_element_type=F32)


def nt(a, b):
    return lax.dot_general(a, b, (((1,), (1,)), ((), ())), preferred_element_type=F32)


def split(x):
    hi = x.astype(BF16)
    return hi, (x - hi.astype(F32)).astype(BF16)


def wide(*parts):
    return jnp.concatenate(parts, axis=1)


def tall(*parts):
    return jnp.concatenate(parts, axis=0)


def kernel(
    blocks, heads, group, sub, q_hbm, k_hbm, v_hbm, w_hbm, beta_hbm, seg_hbm, visit_hbm, out_ref,
    q_ref, k_ref, v_ref, w_ref, beta_ref, seg_ref, visit_ref,
    far_in, far_out, val_in, relay_buf, hub_buf, back, coef, rnorm, beta_rows, turned, own, tops, sums, bias,
    far_send, far_recv, own_send, val_recv, relay_send, relay_recv, hub_send, hub_recv,
    pair_send, pair_recv, skip_sems, load_sem, small_sem, clear_sem,
):
    length = q_ref.shape[0]
    width = q_ref.shape[1] // heads
    depth = far_in.shape[0]
    groups = heads // group
    scale = width ** (-0.5)
    me = lax.axis_index("seq")
    odd = lax.rem(me, 2) == 1
    even = lax.rem(me, 2) == 0
    chip = lax.div(me, 2)
    chips = blocks // 2
    near_side = lax.rem(chip, 2) == 0
    far_side = lax.rem(chip, 2) == 1
    has_left = me >= 1
    has_right = me + 1 < blocks
    onward = chip + 1 < chips
    bent = odd & far_side & onward
    skips = odd & (chip + 2 < chips)
    relays = skips & near_side
    detour = even & far_side & onward
    clears = bent & (chip >= 3)
    held = far_side & (chip + 3 < chips)
    late = min(1, groups - 1)
    rejoined = even & near_side & (chip >= 2)
    follows = even & (chip >= 1)
    skipped = even & (chip >= 2)

    barrier = pltpu.get_barrier_semaphore()

    def greet(cond, other):
        @pl.when(cond)
        def _():
            pl.semaphore_signal(barrier, inc=1, device_id={"seq": other}, device_id_type=MESH)

    turns = range(1, chips - 1, 2)
    for c in turns:
        greet(me == 0, 2 * c)
    for cond, other in (
        (has_left, me - 1),
        (follows, me - 2),
        (relays, me + 2),
        (skipped, me - 3),
        (rejoined, 0),
        (held & odd, me + 4),
        (held & even, me + 5),
    ):
        greet(cond, other)
    loads = [
        pltpu.make_async_copy(src, dst, load_sem.at[i])
        for i, (src, dst) in enumerate(
            ((w_hbm, w_ref), (k_hbm, k_ref), (q_hbm, q_ref), (v_hbm, v_ref))
        )
    ]
    loads[3].start()
    loads[0].start()
    loads[1].start()
    smalls = [
        pltpu.make_async_copy(src, dst, small_sem.at[i])
        for i, (src, dst) in enumerate(
            ((beta_hbm, beta_ref), (seg_hbm, seg_ref), (visit_hbm, visit_ref))
        )
    ]
    for copy in smalls:
        copy.start()

    targets = (has_right, even & onward, bent, skips, detour, clears, clears)
    targets = targets + (me == 0,) * len(turns)

    @pl.when(has_right)
    def _():
        pl.semaphore_wait(barrier, sum(c.astype(jnp.int32) for c in targets))

    loads[3].wait()

    chunk = length // groups

    def remote(src, dst, send, recv, target):
        return pltpu.make_async_remote_copy(
            src_ref=src, dst_ref=dst, send_sem=send, recv_sem=recv,
            device_id={"seq": target}, device_id_type=MESH,
        )

    def rows_of(c):
        return pl.ds(c * chunk, chunk)

    def straight_copy(c, slot, target):
        return remote(
            v_ref.at[rows_of(c)], val_in.at[slot, rows_of(c)],
            own_send.at[c], val_recv.at[slot, c], target,
        )

    def bent_copy(c):
        return remote(
            v_hbm.at[rows_of(c)], relay_buf.at[rows_of(c)],
            own_send.at[c], relay_recv.at[c], me - 2,
        )

    def relay_copy(c):
        return remote(
            relay_buf.at[rows_of(c)], val_in.at[0, rows_of(c)],
            relay_send.at[c], val_recv.at[0, c], me + 3,
        )

    def pair_copy(src, slot):
        return remote(src, val_in.at[slot], pair_send.at[slot], pair_recv.at[slot], me + 1)

    pairs = [pair_copy(v_ref, 0), pair_copy(val_in.at[0], 1), pair_copy(val_in.at[1], 2)]
    skip = remote(v_hbm, val_in.at[2], skip_sems.at[0], skip_sems.at[1], me + 3)

    final = groups - 1

    def detour_copy(i):
        return remote(
            v_ref.at[rows_of(final)], hub_buf.at[i],
            own_send.at[final], hub_recv.at[i], 0,
        )

    def rejoin_copy(i, c):
        return remote(
            hub_buf.at[i], val_in.at[1, rows_of(final)],
            hub_send.at[i], val_recv.at[1, final], 2 * c + 2,
        )

    def relay_on(c):
        @pl.when(relays)
        def _():
            bent_copy(c).wait_recv()
            relay_copy(c).start()

    def size_of(slot):
        return sub if slot == depth - 1 else group

    def far_copy(slot, p):
        part = pl.ds(p * size_of(slot), size_of(slot))
        return pltpu.make_async_remote_copy(
            src_ref=far_out.at[slot, part], dst_ref=far_in.at[slot, part],
            send_sem=far_send.at[slot, p], recv_sem=far_recv.at[slot, p],
            device_id={"seq": me + 1}, device_id_type=MESH,
        )

    ratio = group // sub

    def far_start(slot, g):
        @pl.when(has_right)
        def _():
            pieces = group // size_of(slot)
            for i in range(pieces):
                far_copy(slot, g * pieces + i).start()

    def far_wait(slot, p):
        @pl.when(has_left)
        def _():
            far_copy(slot, p).wait_recv()

    @pl.when(odd & near_side & onward)
    def _():
        for c in range(groups):
            straight_copy(c, 0, me + 1).start()

    @pl.when(detour)
    def _():
        detour_copy(lax.div(chip, 2)).start()
        for c in range(min(1, final)):
            straight_copy(c, 1, me + 2).start()

    @pl.when(even & near_side & onward)
    def _():
        for c in range(groups):
            straight_copy(c, 1, me + 2).start()

    @pl.when(bent)
    def _():
        for c in range(groups):
            bent_copy(c).start()

    @pl.when(skips)
    def _():
        skip.start()

    @pl.when(even)
    def _():
        pairs[0].start()

    loads[2].start()

    @pl.when(me == 0)
    def _():
        far_in[...] = jnp.zeros_like(far_in)
        val_in[0] = jnp.zeros_like(val_in[0])
        val_in[1] = jnp.zeros_like(val_in[1])

    @pl.when(even & (chip < 2))
    def _():
        val_in[2] = jnp.zeros_like(val_in[2])

    rows = lax.broadcasted_iota(jnp.int32, (length, length), 0)
    lanes = lax.broadcasted_iota(jnp.int32, (length, length), 1)
    eye_f = (rows == lanes).astype(F32)
    eye_b = eye_f.astype(BF16)
    for copy in smalls:
        copy.wait()
    beta_rows[...] = beta_ref[...].astype(F32)

    seg_own = seg_ref[pl.ds(me, 1), :].astype(F32)
    seg_col = jnp.sum(jnp.where(rows == lanes, seg_own, 0.0), axis=1, keepdims=True)
    bias[0] = jnp.where((seg_own == seg_col) & (lanes <= rows), 0.0, -1e30)
    for r in range(1, depth + 1):
        seg_far = seg_ref[pl.ds(jnp.maximum(me - r, 0), 1), :].astype(F32)
        seen = jnp.where(visit_ref[0, r - 1] > 0, 0.0, -1e30) + jnp.where(me >= r, 0.0, -1e30)
        bias[r] = jnp.where(seg_far == seg_col, 0.0, -1e30) + seen

    def cols(h):
        return pl.ds(pl.multiple_of(h * width, width), width)

    def heads_of(g):
        return [g * group + i for i in range(group)]

    def prepare(g, carry):
        hs = heads_of(g)
        diag = rows == lanes
        ws = [w_ref[:, cols(h)] for h in hs]
        ks = [k_ref[:, cols(h)] for h in hs]
        grams = [nt(w, w) for w in ws]
        crosses = [nt(k, w) for k, w in zip(ks, ws)]
        rns = [
            1.0 / jnp.sqrt(jnp.sum(jnp.where(diag, m, 0.0), axis=0, keepdims=True) + EPSILON)
            for m in grams
        ]
        arows = [beta_rows[pl.ds(h, 1), :] * rn for h, rn in zip(hs, rns)]
        acols = [jnp.sum(jnp.where(diag, a, 0.0), axis=1, keepdims=True) for a in arows]
        lows = [
            jnp.where(rows > lanes, m * a * rn, 0.0) for m, a, rn in zip(grams, acols, rns)
        ]
        apart = rows ^ lanes
        xs = [eye_f - jnp.where(apart == 1, n, 0.0) for n in lows]
        step = 2
        while step < length:
            here = (apart >= step) & (apart < 2 * step)
            halves = [x.astype(BF16) for x in xs]
            lefts = [
                nn(x, jnp.where(here, n, 0.0).astype(BF16)) for x, n in zip(halves, lows)
            ]
            xs = [x - nn(y.astype(BF16), xb) for x, y, xb in zip(xs, lefts, halves)]
            step = step * 2
        halves = [x.astype(BF16) for x in xs]
        pairs = [split(n) for n in lows]
        rests = [
            (eye_f - xb.astype(F32)) - nn(wide(hi, lo), tall(xb, xb))
            for xb, (hi, lo) in zip(halves, pairs)
        ]
        fulls = [xb.astype(F32) + nn(xb, r.astype(BF16)) for xb, r in zip(halves, rests)]
        ms = [split(x * a) for x, a in zip(fulls, arows)]
        bs = [nn(wide(hi, lo), tall(w, w)) for (hi, lo), w in zip(ms, ws)]
        k2 = [split(jnp.where(lanes > rows, c, 0.0)) for c in crosses]
        cs = [
            nt(wide(chi, clo), wide(hi, hi)) + nt(chi, lo)
            for (chi, clo), (hi, lo) in zip(k2, ms)
        ]
        ds = [split(c * rn) for c, rn in zip(cs, rns)]
        moved = [
            k.astype(F32) - nn(wide(hi, lo), tall(w, w))
            for k, (hi, lo), w in zip(ks, ds, ws)
        ]
        for h, b, c, rn, m in zip(hs, bs, cs, rns, moved):
            far_out[0, h] = m.astype(BF16)
            back[h] = wide(*split(b))
            coef[h] = c
            rnorm[pl.ds(h, 1), :] = rn

        @pl.when(even | jnp.logical_not(held) | (g > late))
        def _():
            far_start(0, g)

        @pl.when(clears & (g == late))
        def _():
            for c in range(final):
                bent_copy(c).wait_send()
            for other in (me - 4, me - 5):
                pl.semaphore_signal(
                    clear_sem, inc=1, device_id={"seq": other}, device_id_type=MESH
                )

        @pl.when(held & (g == late))
        def _():
            pl.semaphore_wait(clear_sem, 1)

        @pl.when(odd & held & (g == late))
        def _():
            for i in range(late + 1):
                far_start(0, i)

        @pl.when(detour & (g == late))
        def _():
            for c in range(1, final):
                straight_copy(c, 1, me + 2).start()

        @pl.when(g >= late)
        def _():
            relay_on(g - late)

        @pl.when((me == 0) & (g == groups // 2))
        def _():
            for i, c in reversed(list(enumerate(turns))):
                detour_copy(i).wait_recv()
                rejoin_copy(i, c).start()

        return carry

    def advance(slot, g):
        hs = heads_of(g)
        far_wait(slot, g)
        fs = [far_in[slot, h] for h in hs]
        inner = [nt(wide(f, f), back[h]) * rnorm[pl.ds(h, 1), :] for f, h in zip(fs, hs)]
        new = [
            f.astype(F32) - nn(y.astype(BF16), w_ref[:, cols(h)])
            for f, y, h in zip(fs, inner, hs)
        ]
        for h, x in zip(hs, new):
            far_out[slot + 1, h] = x.astype(BF16)
        far_start(slot + 1, g)

    def query(g):
        hs = heads_of(g)
        qs = [q_ref[:, cols(h)] for h in hs]
        gs = [
            split(jnp.where(lanes <= rows, nt(q, w_ref[:, cols(h)]) * rnorm[pl.ds(h, 1), :], 0.0))
            for q, h in zip(qs, hs)
        ]
        base = [nt(q, k_ref[:, cols(h)]) for q, h in zip(qs, hs)]
        for h, q, (hi, lo), s in zip(hs, qs, gs, base):
            b = back[h]
            bhi, blo = b[:, :width], b[:, width:]
            t = q.astype(F32) - (nn(wide(hi, lo), tall(bhi, bhi)) + nn(hi, blo))
            turned[h] = wide(*split(t * scale))
            chi, clo = split(coef[h])
            o = s - (nt(wide(hi, lo), wide(chi, chi)) + nt(hi, clo))
            own[h] = o * scale + bias[0]

    loads[0].wait()
    loads[1].wait()
    lax.fori_loop(0, groups, prepare, 0)


    def start(g):
        near = depth - 1
        for h in heads_of(g):
            t = turned[h]
            parts = [own[h]]
            for r in range(near):
                f = far_in[r, h]
                parts.append(nt(t, wide(f, f)) + bias[r + 1])
            top = jnp.max(functools.reduce(jnp.maximum, parts), axis=1, keepdims=True)
            ws = [jnp.exp(p - top) for p in parts]
            total = jnp.sum(functools.reduce(jnp.add, ws), axis=1, keepdims=True)
            tops[h] = jnp.broadcast_to(top, (length, width))
            sums[h] = jnp.broadcast_to(total, (length, width))
            vals = [v_ref[:, cols(h)]] + [val_in[r, :, cols(h)] for r in range(near)]
            own[h] = nn(wide(*[x.astype(BF16) for x in ws]), tall(*vals))

    def share_values(slot):
        @pl.when(even & has_left)
        def _():
            for c in range(groups):
                straight_copy(c, slot, me).wait_recv()

        @pl.when(even)
        def _():
            pairs[slot + 1].start()

    def first_hop(g, carry):
        query(g)
        advance(0, g)

        @pl.when(g < late)
        def _():
            relay_on(g + groups - late)

        return carry

    def second_hop(g, carry):
        advance(1, g)

        @pl.when(g == late)
        def _():
            share_values(1)

        @pl.when(odd & (g == late))
        def _():
            pairs[0].wait_recv()
            pairs[1].wait_recv()

        @pl.when(g >= 1)
        def _():
            start(g - 1)

        return carry

    loads[2].wait()
    lax.fori_loop(0, groups, first_hop, 0)
    share_values(0)
    lax.fori_loop(0, groups, second_hop, 0)
    start(groups - 1)

    @pl.when(skipped)
    def _():
        skip.wait_recv()

    @pl.when(odd)
    def _():
        pairs[2].wait_recv()

    def finish(hs):
        last = depth - 1
        fs = [far_in[last, h] for h in hs]
        ss = [nt(turned[h], wide(f, f)) + bias[depth] for h, f in zip(hs, fs)]
        olds = [tops[h] for h in hs]
        news = [
            jnp.maximum(old, jnp.max(s, axis=1, keepdims=True)) for old, s in zip(olds, ss)
        ]
        ws = [jnp.exp(s - top) for s, top in zip(ss, news)]
        keeps = [jnp.exp(old - top) for old, top in zip(olds, news)]
        adds = [nn(w.astype(BF16), val_in[last, :, cols(h)]) for w, h in zip(ws, hs)]
        for h, w, keep, add in zip(hs, ws, keeps, adds):
            total = sums[h] * keep + jnp.sum(w, axis=1, keepdims=True)
            out_ref[:, cols(h)] = ((own[h] * keep + add) / total).astype(BF16)

    def finish_group(g, carry):
        for i in range(ratio):
            far_wait(depth - 1, g * ratio + i)
        finish(heads_of(g))
        return carry

    def finish_part(p, carry):
        far_wait(depth - 1, p)
        finish([p * sub + i for i in range(sub)])
        return carry

    lax.fori_loop(0, groups - 1, finish_group, 0)
    lax.fori_loop((groups - 1) * ratio, groups * ratio, finish_part, 0)

    @pl.when(has_right)
    def _():
        for slot in range(depth):
            for p in range(heads // size_of(slot)):
                far_copy(slot, p).wait_send()

    @pl.when(onward & jnp.logical_not(clears))
    def _():
        for c in range(final):
            bent_copy(c).wait_send()

    @pl.when(onward)
    def _():
        bent_copy(final).wait_send()

    @pl.when(relays)
    def _():
        for c in range(groups):
            relay_copy(c).wait_send()

    @pl.when(me == 0)
    def _():
        for i, c in enumerate(turns):
            rejoin_copy(i, c).wait_send()

    @pl.when(skips)
    def _():
        skip.wait_send()

    @pl.when(even)
    def _():
        for copy in pairs:
            copy.wait_send()


def solution(mesh):
    blocks = mesh.shape["seq"]

    def shards(queries, keys, values, transitions, betas, segments, visits):
        length, total = queries.shape
        heads = betas.shape[1]
        width = total // heads
        depth = visits.shape[1]
        group = 4 if heads % 4 == 0 else 1
        sub = 2 if group % 2 == 0 else 1
        parts = heads // sub
        groups = heads // group
        turns = max(1, len(range(1, blocks // 2 - 1, 2)))
        anywhere = pl.BlockSpec(memory_space=pl.ANY)
        whole = pl.BlockSpec(memory_space=pltpu.VMEM)
        return pl.pallas_call(
            functools.partial(kernel, blocks, heads, group, sub),
            out_shape=pltpu.VMEM((length, total), BF16),
            in_specs=[anywhere] * 7,
            out_specs=whole,
            scratch_shapes=[pltpu.VMEM((length, total), BF16)] * 4 + [
                pltpu.VMEM((heads, length), BF16),
                pltpu.VMEM((blocks, length), jnp.int32),
                pltpu.SMEM((1, depth), jnp.int32),
                pltpu.VMEM((depth, heads, length, width), BF16),
                pltpu.VMEM((depth, heads, length, width), BF16),
                pltpu.VMEM((depth, length, total), BF16),
                pltpu.VMEM((length, total), BF16),
                pltpu.VMEM((turns, length // groups, total), BF16),
                pltpu.VMEM((heads, length, 2 * width), BF16),
                pltpu.VMEM((heads, length, length), F32),
                pltpu.VMEM((heads, length), F32),
                pltpu.VMEM((heads, length), F32),
                pltpu.VMEM((heads, length, 2 * width), BF16),
                pltpu.VMEM((heads, length, length), F32),
                pltpu.VMEM((heads, length, width), F32),
                pltpu.VMEM((heads, length, width), F32),
                pltpu.VMEM((depth + 1, length, length), F32),
                pltpu.SemaphoreType.DMA((depth, parts)),
                pltpu.SemaphoreType.DMA((depth, parts)),
                pltpu.SemaphoreType.DMA((groups,)),
                pltpu.SemaphoreType.DMA((depth, groups)),
                pltpu.SemaphoreType.DMA((groups,)),
                pltpu.SemaphoreType.DMA((groups,)),
                pltpu.SemaphoreType.DMA((turns,)),
                pltpu.SemaphoreType.DMA((turns,)),
                pltpu.SemaphoreType.DMA((depth,)),
                pltpu.SemaphoreType.DMA((depth,)),
                pltpu.SemaphoreType.DMA((2,)),
                pltpu.SemaphoreType.DMA((4,)),
                pltpu.SemaphoreType.DMA((3,)),
                pltpu.SemaphoreType.REGULAR,
            ],
            compiler_params=pltpu.CompilerParams(collective_id=0, has_side_effects=True),
        )(
            queries, keys, values, transitions, betas.T,
            segments.reshape(-1, length), visits,
        )

    return jax.shard_map(
        shards,
        mesh=mesh,
        in_specs=(
            P("seq", "head"),
            P("seq", "head"),
            P("seq", "head"),
            P("seq", "head"),
            P("seq", "head"),
            P(),
            P("seq", None),
        ),
        out_specs=P("seq", "head"),
        check_vma=False,
    )
```
